512 devices in a mesh: row: 32 (over y, x, core), col: 16 (over z).
Axes of the slice: x: 4, y: 4, z: 16, core: 2. Of those that a mesh axis runs over, the one named last changes fastest.
Arguments:
- front: float32 [4, 32, 128, 8, 16, 128], P(None, 'row', None, None, 'col'), may hold values from 0 to 1, as said below
- support: float32 [4, 32, 128], P(None, 'row'), may hold values from 0.5 to 2
- mask: int32 [128, 128], replicated, may hold values from 0 to 1, as said below
- rhs: float32 [512, 4, 32, 128], P('col', None, 'row'), may hold values from -6 to 6
Outputs:
- factor: float32 [4, 32, 128, 8, 16, 128], P(None, 'row', None, None, 'col')
- solved: float32 [512, 4, 32, 128], P('col', None, 'row')
The draws below stay inside these ranges and needn't reach their ends.
Inputs may be any that keep to these rules, and one draw needn't show every extreme that they name: mask[I, J] is 1 exactly when block rows I and J carry the same one of three subtree labels; it is symmetric with ones on the diagonal. front is symmetric and positive semidefinite with ones on its diagonal.
All inputs are finite; a program needn't handle non-finite values.
Results may differ from the reference program's by a relative error of at most 0.000057.
Values sent between devices are 32-bit elements; how exact they have to be, the bound alone decides.
No kernel may reach another device: no remote copies, remote signals or barrier semaphores. Data moves between devices by JAX's collectives and lax.ppermute only.
A program may use at most 64 MiB of HBM per device.

```python
import math
import jax
import jax.numpy as jnp
from jax import lax

BLOCK = 128
BR_DEV = 4
KB = 3
R = 512
M = 16384
BC_DEV = 8
NB = 128
N_ROW = 32
N_COL = 16


def draw_front(key, part):
    coords = jax.random.uniform(jax.random.fold_in(key, 11), (3, M), jnp.float32)
    length_scale = 0.4
    offset_one = coords[0][:, None] - coords[0][None, :]
    offset_two = coords[1][:, None] - coords[1][None, :]
    offset_three = coords[2][:, None] - coords[2][None, :]
    distance = jnp.sqrt(offset_one * offset_one + offset_two * offset_two + offset_three * offset_three)
    kernel = jnp.exp(-distance / length_scale)
    return kernel.reshape(BR_DEV, N_ROW, BLOCK, BC_DEV, N_COL, BLOCK)


def draw_mask(key, part):
    labels = jax.random.randint(jax.random.fold_in(key, 23), (NB,), 0, 3)
    return (labels[:, None] == labels[None, :]).astype(jnp.int32)


def steps_of(own_key, dims, shards, least, top_value):
    factor_of = 1.0
    for position, shards_of in shards:
        steps = jax.random.uniform(jax.random.fold_in(jax.random.fold_in(own_key, 6), position), (shards_of,), jnp.float32, least / len(shards), top_value / len(shards))
        factor_of = factor_of * jnp.repeat(jnp.exp(steps), dims[position] // shards_of).reshape((-1,) + (1,) * (len(dims) - 1 - position))
    return factor_of


def scatter_about(rng, extent, spread, bound, pieces=(), dtype=jnp.bfloat16):
    factor_of = steps_of(rng, extent, pieces, -0.22, 0.18) if pieces else 1.0
    array = jax.random.normal(rng, extent, jnp.float32) * spread * factor_of
    return jnp.minimum(jnp.maximum(array, -bound), bound).astype(dtype)


def setup_inputs(seed: int = 0) -> dict:
    splits = jax.random.split(jax.random.key(seed), 5)
    return {
        "front": draw_front(jax.random.fold_in(splits[4], 71), 0),
        "support": jnp.clip(jnp.exp(math.log(2.0) - 1.3862944 * jax.random.uniform(splits[1], (BR_DEV, N_ROW, BLOCK), jnp.float32) ** steps_of(splits[1], (BR_DEV, N_ROW, BLOCK), ((1, 32),), -0.2, 0.2)), 0.5, 2.0),
        "mask": draw_mask(jax.random.fold_in(splits[4], 71), 0),
        "rhs": scatter_about(splits[3], (R, BR_DEV, N_ROW, BLOCK), 1.0, 6.0, ((0, 16), (2, 32)), jnp.float32),
    }


def reference(front, support, mask, rhs):
    precise = lax.Precision.HIGHEST
    dense_front = front.reshape(M, M)
    pattern = jnp.repeat(jnp.repeat(mask.astype(jnp.float32), BLOCK, axis=0), BLOCK, axis=1)
    matrix = dense_front * pattern + jnp.diag(support.reshape(M))
    eliminated = KB * BLOCK
    diag_factor = jnp.linalg.cholesky(matrix[:eliminated, :eliminated])
    below_rows = jax.scipy.linalg.solve_triangular(diag_factor, matrix[eliminated:, :eliminated].T, lower=True).T
    schur_part = matrix[eliminated:, eliminated:] - jnp.dot(below_rows, below_rows.T, precision=precise)
    result = jnp.zeros((M, M), jnp.float32)
    result = result.at[:eliminated, :eliminated].set(diag_factor)
    result = result.at[eliminated:, :eliminated].set(below_rows)
    result = result.at[eliminated:, eliminated:].set(schur_part)
    factor = result.reshape(BR_DEV, N_ROW, BLOCK, BC_DEV, N_COL, BLOCK)
    rhs_cols = rhs.reshape(R, M).T
    top_rows = jax.scipy.linalg.solve_triangular(diag_factor, rhs_cols[:eliminated], lower=True)
    rest_rows = rhs_cols[eliminated:] - jnp.dot(below_rows, top_rows, precision=precise)
    solved = jnp.concatenate([top_rows, rest_rows], axis=0).T.reshape(R, BR_DEV, N_ROW, BLOCK)
    return (factor, solved)
```

```python
import jax
import jax.numpy as jnp
from jax import lax
from jax.sharding import PartitionSpec as P

KB = 3


precise = lax.Precision.HIGHEST


def mm(a, b):
    return jnp.dot(a, b, precision=precise, preferred_element_type=jnp.float32)


def shards(front, support, mask, rhs):
    n_row = lax.axis_size("row")
    n_col = lax.axis_size("col")
    p = lax.axis_index("row")
    q = lax.axis_index("col")
    rows_dev = front.shape[0]
    blk = front.shape[2]
    cols_dev = front.shape[3]
    halves = n_row // n_col
    sub = blk // n_row
    row_ids = jnp.arange(rows_dev, dtype=jnp.int32) * n_row + p
    col_ids = jnp.arange(cols_dev, dtype=jnp.int32) * n_col + q
    mask_rows = lax.dynamic_index_in_dim(mask.reshape(rows_dev, n_row, -1), p, 1, keepdims=False)
    pattern = lax.dynamic_index_in_dim(
        mask_rows.reshape(rows_dev, cols_dev, n_col), q, 2, keepdims=False
    ).astype(jnp.float32)
    on_diag = (row_ids[:, None] == col_ids[None, :]).astype(jnp.float32)
    x = front[:, 0, :, :, 0, :]
    eye = jnp.eye(blk, dtype=jnp.float32)
    diag_add = support[:, 0, :][:, :, None] * eye[None]
    matrix = x * pattern[:, None, :, None] + on_diag[:, None, :, None] * diag_add[:, :, None, :]
    values = rhs[:, :, 0, :]

    top = matrix[0].reshape(n_row, sub * cols_dev, blk)
    sent = jnp.concatenate([top, values[:, 0, :].reshape(n_row, -1, blk)], axis=1)
    got = lax.all_to_all(sent, "row", 0, 0)[:KB]
    mine = got[:, : sub * cols_dev]
    mine_rhs = got[:, sub * cols_dev :]
    every = lax.all_gather(mine, "col")
    every = every.reshape(n_col, KB, sub, rows_dev, halves, blk)
    to_rows = every.transpose(4, 0, 1, 2, 3, 5).reshape(n_row, KB * sub * rows_dev, blk)
    diag_part = every[:KB, :, :, 0, 0].transpose(1, 2, 0, 3).reshape(KB * sub * KB, blk)
    shared = jnp.concatenate([mine.reshape(-1, blk), diag_part, mine_rhs.reshape(-1, blk)], axis=0)
    sent = jnp.concatenate(
        [to_rows, jnp.broadcast_to(shared[None], (n_row,) + shared.shape)], axis=1
    )
    got = lax.all_to_all(sent, "row", 0, 0)
    size = KB * blk

    def lay(part, wide):
        part = part.reshape(n_row, KB, sub, wide, blk)
        return part.transpose(1, 0, 2, 3, 4).reshape(size, wide * blk)

    ends = [KB * sub * rows_dev, KB * sub * cols_dev, KB * sub * KB, KB * mine_rhs.shape[1]]
    at = [0]
    for e in ends:
        at.append(at[-1] + e)
    row_panel = lay(got[:, at[0] : at[1]], rows_dev)
    col_panel = lay(got[:, at[1] : at[2]], cols_dev)
    diag = lay(got[:, at[2] : at[3]], KB)
    first_rhs = got[:, at[3] : at[4]].reshape(n_row, KB, -1, blk).transpose(0, 2, 1, 3)
    first_rhs = first_rhs.reshape(values.shape[0], size)

    factor = jnp.linalg.cholesky(diag)
    inverse = jax.scipy.linalg.solve_triangular(factor, jnp.eye(size, dtype=jnp.float32), lower=True)
    row_solved = mm(inverse, row_panel)
    col_solved = mm(inverse, col_panel)
    found = lax.dot_general(
        first_rhs, inverse, (((1,), (1,)), ((), ())), precision=precise
    )

    update = lax.dot_general(
        row_solved.reshape(size, rows_dev, blk),
        col_solved.reshape(size, cols_dev, blk),
        (((0,), (0,)), ((), ())),
        precision=precise,
    )
    schur = matrix - update
    own_l11 = lax.dynamic_index_in_dim(
        lax.dynamic_index_in_dim(
            factor.reshape(KB, blk, KB, blk), jnp.minimum(p, KB - 1), 0, keepdims=False
        ),
        jnp.minimum(q, KB - 1),
        1,
        keepdims=False,
    )
    own_l21 = lax.dynamic_index_in_dim(
        row_solved.reshape(KB, blk, rows_dev, blk), jnp.minimum(q, KB - 1), 0, keepdims=False
    ).transpose(1, 2, 0)
    low = (row_ids < KB)[:, None, None, None]
    left = (col_ids < KB)[None, None, :, None]
    panel = jnp.where((row_ids < KB)[:, None, None], own_l11[None], own_l21)[:, :, None, :]
    result = jnp.where(left, panel, jnp.where(low, 0.0, schur))

    rest = values - mm(found, row_solved).reshape(values.shape)
    own_y1 = lax.dynamic_index_in_dim(
        found.reshape(-1, KB, blk), jnp.minimum(p, KB - 1), 1, keepdims=False
    )
    solved = jnp.where((row_ids < KB)[None, :, None], own_y1[:, None, :], rest)
    return (result.reshape(front.shape), solved.reshape(rhs.shape))


def solution(mesh):
    placed = (
        P(None, "row", None, None, "col", None),
        P(None, "row", None),
        P(),
        P("col", None, "row", None),
    )
    return jax.shard_map(
        shards,
        mesh=mesh,
        in_specs=placed,
        out_specs=(P(None, "row", None, None, "col", None), P("col", None, "row", None)),
        check_vma=False,
    )
```

```python
import jax
import jax.numpy as jnp
from jax import lax
from jax.experimental import pallas as pl
from jax.experimental.pallas import tpu as pltpu
from jax.sharding import PartitionSpec as P

KB = 3
SPAN = 32
STEP = 8

precise = lax.Precision.HIGHEST


def tdot(a, b):
    return lax.dot_general(
        a, b, (((0,), (0,)), ((), ())), precision=precise, preferred_element_type=jnp.float32
    )


def ndot(a, b):
    return jnp.dot(a, b, precision=precise, preferred_element_type=jnp.float32)


def rdot(a, b):
    return lax.dot_general(
        a, b, (((1,), (1,)), ((), ())), precision=precise, preferred_element_type=jnp.float32
    )


def spread(x, row):
    return jnp.broadcast_to(x[row : row + 1, :], x.shape)


def eliminate_diagonal(aug_ref):
    blk = aug_ref.shape[0]
    sub = lax.broadcasted_iota(jnp.int32, (STEP, blk), 0)
    parts = SPAN // STEP
    for g in range(blk // SPAN):
        base = g * SPAN
        rows = [slice(base + STEP * j, base + STEP * (j + 1)) for j in range(parts)]
        left = [aug_ref[rows[j], :blk] for j in range(parts)]
        right = [aug_ref[rows[j], blk:] for j in range(parts)]
        for i in range(parts):
            c0 = base + STEP * i
            cols = [
                jnp.broadcast_to(left[i][:, c0 + u : c0 + u + 1], (STEP, blk)) for u in range(STEP)
            ]
            pivots = jnp.ones((STEP, blk), jnp.float32)
            inv = []
            tops = {}
            for t in range(STEP):
                pivot = spread(cols[t], t)
                pivots = jnp.where(sub == t, pivot, pivots)
                inv.append(1.0 / pivot)
                ratio = jnp.where(sub > t, cols[t] * inv[t], 0.0)
                for u in range(t + 1, STEP):
                    tops[t, u] = spread(cols[u], t)
                    cols[u] = cols[u] - ratio * tops[t, u]
                left[i] = left[i] - ratio * spread(left[i], t)
                right[i] = right[i] - ratio * spread(right[i], t)
            for j in range(i + 1, parts):
                below = [
                    jnp.broadcast_to(left[j][:, c0 + u : c0 + u + 1], (STEP, blk))
                    for u in range(STEP)
                ]
                for t in range(STEP):
                    ratio = below[t] * inv[t]
                    for u in range(t + 1, STEP):
                        below[u] = below[u] - ratio * tops[t, u]
                    left[j] = left[j] - ratio * spread(left[i], t)
                    right[j] = right[j] - ratio * spread(right[i], t)
            scale = lax.rsqrt(pivots)
            left[i] = left[i] * scale
            right[i] = right[i] * scale
        for j in range(parts):
            aug_ref[rows[j], :blk] = left[j]
            aug_ref[rows[j], blk:] = right[j]
        end = base + SPAN
        if end < blk:
            done = aug_ref[base:end, :]
            term = tdot(done[:, :blk], done)
            aug_ref[end:, :] = aug_ref[end:, :] - term[end:, :]


def factor_kernel(diag_ref, cols_ref, inv_ref, col_ref, found_ref, a_ref, c_ref, aug_ref):
    blk = aug_ref.shape[0]
    size = inv_ref.shape[0]
    wide = col_ref.shape[1] // blk
    count = found_ref.shape[0]
    pitch = KB * KB + 1
    for k in range(KB):
        for j in range(k, KB):
            a_ref[k * blk : (k + 1) * blk, j * blk : (j + 1) * blk] = diag_ref[
                pl.ds(k * KB + j, blk, stride=pitch), :
            ]
    inv_ref[...] = jnp.zeros(inv_ref.shape, jnp.float32)
    eye = lax.broadcasted_iota(jnp.int32, (blk, blk), 0) == lax.broadcasted_iota(
        jnp.int32, (blk, blk), 1
    )
    for k in range(KB):
        k0, k1 = k * blk, (k + 1) * blk
        aug_ref[:, :blk] = a_ref[k0:k1, k0:k1]
        aug_ref[:, blk:] = eye.astype(jnp.float32)
        eliminate_diagonal(aug_ref)
        own = aug_ref[:, blk:]
        if k > 0:
            inv_ref[k0:k1, :k0] = ndot(own, inv_ref[k0:k1, :k0])
        inv_ref[k0:k1, k0:k1] = own
        if k1 < size:
            up = ndot(own, a_ref[k0:k1, k1:])
            a_ref[k1:, k1:] = a_ref[k1:, k1:] - tdot(up, up)
            inv_ref[k1:, :k1] = inv_ref[k1:, :k1] - tdot(up, inv_ref[k0:k1, :k1])
    for k in range(KB):
        for m in range(wide):
            c_ref[k * blk : (k + 1) * blk, m * blk : (m + 1) * blk] = cols_ref[
                pl.ds(k * wide + m, blk, stride=KB * wide), :
            ]
    for k in range(KB):
        k0, k1 = k * blk, (k + 1) * blk
        col_ref[k0:k1, :] = ndot(inv_ref[k0:k1, :k1], c_ref[:k1, :])
    first = jnp.concatenate(
        [
            diag_ref[pl.ds(k * pitch + pitch - 1, count, stride=diag_ref.shape[0] // count), :]
            for k in range(KB)
        ],
        axis=1,
    )
    found_ref[...] = rdot(first, inv_ref[...])


def finish_kernel(
    where_ref, pattern_ref, x_ref, support_ref, rhs_ref, rows_ref, inv_ref, col_ref, found_ref,
    out_ref, solved_ref, t_ref, s_ref,
):
    step = pl.program_id(0)
    p = where_ref[0]
    q = where_ref[1]
    n_row = where_ref[2]
    n_col = where_ref[3]
    blk = support_ref.shape[1]
    rows_dev = support_ref.shape[0]
    wide = col_ref.shape[1] // blk
    count = found_ref.shape[0]

    @pl.when(step == 0)
    def _():
        for k in range(KB):
            for l in range(rows_dev):
                t_ref[k * blk : (k + 1) * blk, l * blk : (l + 1) * blk] = rows_ref[
                    pl.ds(k * rows_dev + l, blk, stride=KB * rows_dev), :
                ]
        for k in range(KB):
            k0, k1 = k * blk, (k + 1) * blk
            got = ndot(inv_ref[k0:k1, :k1], t_ref[:k1, :])
            for l in range(rows_dev):
                s_ref[l, k0:k1, :] = got[:, l * blk : (l + 1) * blk]
        for l in range(rows_dev):
            rest = rhs_ref[pl.ds(l, count, stride=rows_dev), :] - ndot(found_ref[...], s_ref[l])
            if l == 0:
                for k in range(KB):
                    rest = jnp.where(p == k, found_ref[:, k * blk : (k + 1) * blk], rest)
            solved_ref[pl.ds(l, count, stride=rows_dev), :] = rest

    ri = lax.broadcasted_iota(jnp.int32, (blk, blk), 0)
    ci = lax.broadcasted_iota(jnp.int32, (blk, blk), 1)
    mine = s_ref[step]
    term = tdot(mine, col_ref[...])
    row_id = step * n_row + p
    diag = jnp.where(ri == ci, jnp.broadcast_to(support_ref[pl.ds(step, 1), :], (blk, blk)), 0.0)
    for m in range(wide):
        col_id = m * n_col + q
        got = x_ref[pl.ds(m, blk, stride=wide), :] * pattern_ref[step * wide + m]
        got = got - term[:, m * blk : (m + 1) * blk]
        got = got + jnp.where(row_id == col_id, diag, 0.0)
        if m == 0:
            piece = mine[:blk, :]
            for k in range(1, KB):
                piece = jnp.where(q == k, mine[k * blk : (k + 1) * blk, :], piece)
            piece = piece.T
            piece = jnp.where((row_id == col_id) & (ri < ci), 0.0, piece)
            got = jnp.where(q < KB, piece, got)
        got = jnp.where((row_id < KB) & (col_id > row_id), 0.0, got)
        out_ref[pl.ds(m, blk, stride=wide), :] = got


def factor_call(diag, cols, wide, count):
    blk = diag.shape[1]
    size = KB * blk
    return pl.pallas_call(
        factor_kernel,
        out_shape=(
            jax.ShapeDtypeStruct((size, size), jnp.float32),
            jax.ShapeDtypeStruct((size, wide * blk), jnp.float32),
            jax.ShapeDtypeStruct((count, size), jnp.float32),
        ),
        scratch_shapes=[
            pltpu.VMEM((size, size), jnp.float32),
            pltpu.VMEM((size, wide * blk), jnp.float32),
            pltpu.VMEM((blk, 2 * blk), jnp.float32),
        ],
        compiler_params=pltpu.CompilerParams(vmem_limit_bytes=40 << 20),
        name="factor",
    )(diag, cols)


def finish_call(place, pattern, x, support, rhs, rows, inv, col, found):
    rows_dev, blk = support.shape
    size = inv.shape[0]
    part = x.shape[0] // rows_dev

    def whole(a):
        return pl.BlockSpec(a.shape, lambda i: (0, 0))

    scalars = pl.BlockSpec(memory_space=pltpu.SMEM)
    tile = pl.BlockSpec((part, blk), lambda i: (i, 0))
    return pl.pallas_call(
        finish_kernel,
        grid=(rows_dev,),
        in_specs=[scalars, scalars, tile, whole(support), whole(rhs), whole(rows), whole(inv),
                  whole(col), whole(found)],
        out_specs=(tile, whole(rhs)),
        out_shape=(
            jax.ShapeDtypeStruct(x.shape, jnp.float32),
            jax.ShapeDtypeStruct(rhs.shape, jnp.float32),
        ),
        scratch_shapes=[
            pltpu.VMEM((size, rows_dev * blk), jnp.float32),
            pltpu.VMEM((rows_dev, size, blk), jnp.float32),
        ],
        compiler_params=pltpu.CompilerParams(vmem_limit_bytes=40 << 20),
        name="finish",
    )(place, pattern, x, support, rhs, rows, inv, col, found)


def shards(front, support, mask, rhs):
    n_row = lax.axis_size("row")
    n_col = lax.axis_size("col")
    p = lax.axis_index("row")
    q = lax.axis_index("col")
    rows_dev = front.shape[0]
    blk = front.shape[2]
    cols_dev = front.shape[3]
    halves = n_row // n_col
    sub = blk // n_row
    count = rhs.shape[0]
    mask_rows = lax.dynamic_index_in_dim(mask.reshape(rows_dev, n_row, -1), p, 1, keepdims=False)
    pattern = lax.dynamic_index_in_dim(
        mask_rows.reshape(rows_dev, cols_dev, n_col), q, 2, keepdims=False
    ).astype(jnp.float32)
    place = jnp.stack([p, q, jnp.int32(n_row), jnp.int32(n_col)])
    x = front.reshape(rows_dev * blk * cols_dev, blk)
    values = rhs.reshape(count, rows_dev, blk)

    top = front[0, 0, :, :, 0, :] * pattern[0][None, :, None]
    shape = top.shape
    a_id = lax.broadcasted_iota(jnp.int32, shape, 0)
    m_id = lax.broadcasted_iota(jnp.int32, shape, 1)
    b_id = lax.broadcasted_iota(jnp.int32, shape, 2)
    at_diag = (a_id == b_id) & (m_id * n_col + q == p)
    top = top + jnp.where(at_diag, support[0, 0][None, None, :], 0.0)
    sent = jnp.concatenate(
        [top.reshape(n_row, sub * cols_dev, blk), values[:, 0, :].reshape(n_row, -1, blk)], axis=1
    )
    got = lax.all_to_all(sent, "row", 0, 0)[:KB]
    mine = got[:, : sub * cols_dev].reshape(KB, sub, cols_dev, blk).transpose(1, 0, 2, 3)
    mine = mine.reshape(sub * KB * cols_dev, blk)
    mine_rhs = got[:, sub * cols_dev :].reshape(KB, blk)

    def to_all(part):
        sent = jnp.broadcast_to(part[None], (n_row,) + part.shape)
        return lax.all_to_all(sent, "row", 0, 0).reshape(-1, blk)

    cols_got = to_all(mine)
    every = lax.all_gather(mine, "col").reshape(n_col, sub, KB, rows_dev, halves, blk)
    diag_part = every[:KB, :, :, 0, 0].transpose(1, 2, 0, 3).reshape(sub, KB * KB, blk)
    rhs_part = jnp.concatenate([mine_rhs, jnp.zeros((sub - KB, blk), jnp.float32)], axis=0)
    diag_part = jnp.concatenate([diag_part, rhs_part[:, None, :]], axis=1)
    diag_got = to_all(diag_part.reshape(-1, blk))
    to_rows = every.transpose(4, 0, 1, 2, 3, 5).reshape(n_row, sub * KB * rows_dev, blk)
    rows_got = lax.all_to_all(to_rows, "row", 0, 0).reshape(-1, blk)

    inv, col, found = factor_call(diag_got, cols_got, cols_dev, count)
    factor, solved = finish_call(
        place, pattern.reshape(-1), x, support[:, 0, :], values.reshape(-1, blk), rows_got, inv,
        col, found,
    )
    return (factor.reshape(front.shape), solved.reshape(rhs.shape))


def solution(mesh):
    placed = (
        P(None, "row", None, None, "col", None),
        P(None, "row", None),
        P(),
        P("col", None, "row", None),
    )
    return jax.shard_map(
        shards,
        mesh=mesh,
        in_specs=placed,
        out_specs=(P(None, "row", None, None, "col", None), P("col", None, "row", None)),
        check_vma=False,
    )
```

```python
import jax
import jax.numpy as jnp
from jax import lax
from jax.experimental import pallas as pl
from jax.experimental.pallas import tpu as pltpu
from jax.sharding import PartitionSpec as P

KB = 3
SPAN = 32
STEP = 8

precise = lax.Precision.HIGHEST


def tdot(a, b):
    return lax.dot_general(
        a, b, (((0,), (0,)), ((), ())), precision=precise, preferred_element_type=jnp.float32
    )


def ndot(a, b):
    return jnp.dot(a, b, precision=precise, preferred_element_type=jnp.float32)


def rdot(a, b):
    return lax.dot_general(
        a, b, (((1,), (1,)), ((), ())), precision=precise, preferred_element_type=jnp.float32
    )


def spread(x, row):
    return jnp.broadcast_to(x[row : row + 1, :], x.shape)


def eliminate_diagonal(aug_ref):
    blk = aug_ref.shape[0]
    sub = lax.broadcasted_iota(jnp.int32, (STEP, blk), 0)
    parts = SPAN // STEP
    for g in range(blk // SPAN):
        base = g * SPAN
        rows = [slice(base + STEP * j, base + STEP * (j + 1)) for j in range(parts)]
        left = [aug_ref[rows[j], :blk] for j in range(parts)]
        right = [aug_ref[rows[j], blk:] for j in range(parts)]
        for i in range(parts):
            c0 = base + STEP * i
            cols = [
                jnp.broadcast_to(left[i][:, c0 + u : c0 + u + 1], (STEP, blk)) for u in range(STEP)
            ]
            pivots = jnp.ones((STEP, blk), jnp.float32)
            inv = []
            tops = {}
            for t in range(STEP):
                pivot = spread(cols[t], t)
                pivots = jnp.where(sub == t, pivot, pivots)
                inv.append(1.0 / pivot)
                ratio = jnp.where(sub > t, cols[t] * inv[t], 0.0)
                for u in range(t + 1, STEP):
                    tops[t, u] = spread(cols[u], t)
                    cols[u] = cols[u] - ratio * tops[t, u]
                left[i] = left[i] - ratio * spread(left[i], t)
                right[i] = right[i] - ratio * spread(right[i], t)
            for j in range(i + 1, parts):
                below = [
                    jnp.broadcast_to(left[j][:, c0 + u : c0 + u + 1], (STEP, blk))
                    for u in range(STEP)
                ]
                for t in range(STEP):
                    ratio = below[t] * inv[t]
                    for u in range(t + 1, STEP):
                        below[u] = below[u] - ratio * tops[t, u]
                    left[j] = left[j] - ratio * spread(left[i], t)
                    right[j] = right[j] - ratio * spread(right[i], t)
            scale = lax.rsqrt(pivots)
            left[i] = left[i] * scale
            right[i] = right[i] * scale
        for j in range(parts):
            aug_ref[rows[j], :blk] = left[j]
            aug_ref[rows[j], blk:] = right[j]
        end = base + SPAN
        if end < blk:
            done = aug_ref[base:end, :]
            term = tdot(done[:, :blk], done)
            aug_ref[end:, :] = aug_ref[end:, :] - term[end:, :]


def factor_kernel(diag_ref, inv_ref, found_ref, a_ref, aug_ref):
    blk = aug_ref.shape[0]
    size = inv_ref.shape[0]
    count = found_ref.shape[0]
    pitch = KB * KB + 1
    for k in range(KB):
        for j in range(k, KB):
            a_ref[k * blk : (k + 1) * blk, j * blk : (j + 1) * blk] = diag_ref[
                pl.ds(k * KB + j, blk, stride=pitch), :
            ]
    inv_ref[...] = jnp.zeros(inv_ref.shape, jnp.float32)
    eye = lax.broadcasted_iota(jnp.int32, (blk, blk), 0) == lax.broadcasted_iota(
        jnp.int32, (blk, blk), 1
    )
    for k in range(KB):
        k0, k1 = k * blk, (k + 1) * blk
        aug_ref[:, :blk] = a_ref[k0:k1, k0:k1]
        aug_ref[:, blk:] = eye.astype(jnp.float32)
        eliminate_diagonal(aug_ref)
        own = aug_ref[:, blk:]
        if k > 0:
            inv_ref[k0:k1, :k0] = ndot(own, inv_ref[k0:k1, :k0])
        inv_ref[k0:k1, k0:k1] = own
        if k1 < size:
            up = ndot(own, a_ref[k0:k1, k1:])
            a_ref[k1:, k1:] = a_ref[k1:, k1:] - tdot(up, up)
            inv_ref[k1:, :k1] = inv_ref[k1:, :k1] - tdot(up, inv_ref[k0:k1, :k1])
    first = jnp.concatenate(
        [
            diag_ref[pl.ds(k * pitch + pitch - 1, count, stride=diag_ref.shape[0] // count), :]
            for k in range(KB)
        ],
        axis=1,
    )
    found_ref[...] = rdot(first, inv_ref[...])


def gather_solve(inv_ref, got_ref, wide, to_ref):
    blk = got_ref.shape[1]
    size = KB * blk
    for k in range(KB):
        for j in range(wide):
            to_ref[k * blk : (k + 1) * blk, j * blk : (j + 1) * blk] = got_ref[
                pl.ds(k * wide + j, blk, stride=KB * wide), :
            ]
    for k in reversed(range(KB)):
        k0, k1 = k * blk, (k + 1) * blk
        to_ref[k0:k1, :] = ndot(inv_ref[k0:k1, :k1], to_ref[:k1, :])


def finish_kernel(
    where_ref, pattern_ref, x_hbm, cols_hbm, support_ref, rhs_ref, rows_ref, inv_ref, found_ref,
    out_hbm, solved_ref, x_ref, cols_ref, out_ref, row_ref, col_ref, in_sem, cols_sem, out_sem,
):
    p = where_ref[0]
    q = where_ref[1]
    n_row = where_ref[2]
    n_col = where_ref[3]
    rows_dev, blk = support_ref.shape
    wide = col_ref.shape[1] // blk
    count = found_ref.shape[0]
    part = blk * wide
    load_cols = pltpu.make_async_copy(cols_hbm, cols_ref, cols_sem)
    load_cols.start()
    load = pltpu.make_async_copy(x_hbm, x_ref, in_sem)
    load.start()
    gather_solve(inv_ref, rows_ref, rows_dev, row_ref)
    rest = ndot(found_ref[...], row_ref[...])
    for l in range(rows_dev):
        got = rhs_ref[pl.ds(l, count, stride=rows_dev), :] - rest[:, l * blk : (l + 1) * blk]
        if l == 0:
            for k in range(KB):
                got = jnp.where(p == k, found_ref[:, k * blk : (k + 1) * blk], got)
        solved_ref[pl.ds(l, count, stride=rows_dev), :] = got

    load_cols.wait()
    gather_solve(inv_ref, cols_ref, wide, col_ref)
    ri = lax.broadcasted_iota(jnp.int32, (blk, blk), 0)
    ci = lax.broadcasted_iota(jnp.int32, (blk, blk), 1)
    load.wait()
    stores = []
    pair = 2
    for g in range(rows_dev // pair):
        term = tdot(row_ref[:, g * pair * blk : (g + 1) * pair * blk], col_ref[...])
        for h in range(pair):
            l = g * pair + h
            mine = row_ref[:, l * blk : (l + 1) * blk]
            row_id = l * n_row + p
            diag = jnp.where(
                ri == ci, jnp.broadcast_to(support_ref[l : l + 1, :], (blk, blk)), 0.0
            )
            for m in range(wide):
                col_id = m * n_col + q
                got = x_ref[pl.ds(l * part + m, blk, stride=wide), :]
                got = got * pattern_ref[l * wide + m]
                got = got - term[h * blk : (h + 1) * blk, m * blk : (m + 1) * blk]
                got = got + jnp.where(row_id == col_id, diag, 0.0)
                if m == 0:
                    piece = mine[:blk, :]
                    for k in range(1, KB):
                        piece = jnp.where(q == k, mine[k * blk : (k + 1) * blk, :], piece)
                    piece = piece.T
                    if l == 0:
                        piece = jnp.where((row_id == col_id) & (ri < ci), 0.0, piece)
                    got = jnp.where(q < KB, piece, got)
                if l == 0:
                    got = jnp.where((row_id < KB) & (col_id > row_id), 0.0, got)
                out_ref[pl.ds(l * part + m, blk, stride=wide), :] = got
        span = pl.ds(g * pair * part, pair * part)
        store = pltpu.make_async_copy(out_ref.at[span, :], out_hbm.at[span, :], out_sem.at[g])
        store.start()
        stores.append(store)
    for store in stores:
        store.wait()


def factor_call(diag, count):
    blk = diag.shape[1]
    size = KB * blk
    return pl.pallas_call(
        factor_kernel,
        out_shape=(
            jax.ShapeDtypeStruct((size, size), jnp.float32),
            jax.ShapeDtypeStruct((count, size), jnp.float32),
        ),
        scratch_shapes=[
            pltpu.VMEM((size, size), jnp.float32),
            pltpu.VMEM((blk, 2 * blk), jnp.float32),
        ],
        compiler_params=pltpu.CompilerParams(vmem_limit_bytes=8 << 20),
        name="factor",
    )(diag)


def finish_call(place, pattern, x, support, rhs, rows, cols, inv, found):
    rows_dev, blk = support.shape
    size = inv.shape[0]
    wide = x.shape[0] // (rows_dev * blk)
    scalars = pl.BlockSpec(memory_space=pltpu.SMEM)
    far = pl.BlockSpec(memory_space=pltpu.HBM)
    near = pl.BlockSpec(memory_space=pltpu.VMEM)
    return pl.pallas_call(
        finish_kernel,
        in_specs=[scalars, scalars, far, far] + [near] * 5,
        out_specs=(far, near),
        out_shape=(
            jax.ShapeDtypeStruct(x.shape, jnp.float32),
            jax.ShapeDtypeStruct(rhs.shape, jnp.float32),
        ),
        scratch_shapes=[
            pltpu.VMEM(x.shape, jnp.float32),
            pltpu.VMEM(cols.shape, jnp.float32),
            pltpu.VMEM(x.shape, jnp.float32),
            pltpu.VMEM((size, rows_dev * blk), jnp.float32),
            pltpu.VMEM((size, wide * blk), jnp.float32),
            pltpu.SemaphoreType.DMA,
            pltpu.SemaphoreType.DMA,
            pltpu.SemaphoreType.DMA((rows_dev // 2,)),
        ],
        compiler_params=pltpu.CompilerParams(vmem_limit_bytes=24 << 20),
        name="finish",
    )(place, pattern, x, cols, support, rhs, rows, inv, found)


def shards(front, support, mask, rhs):
    n_row = lax.axis_size("row")
    n_col = lax.axis_size("col")
    p = lax.axis_index("row")
    q = lax.axis_index("col")
    rows_dev = front.shape[0]
    blk = front.shape[2]
    cols_dev = front.shape[3]
    halves = n_row // n_col
    sub = blk // n_row
    count = rhs.shape[0]
    mask_rows = lax.dynamic_index_in_dim(mask.reshape(rows_dev, n_row, -1), p, 1, keepdims=False)
    pattern = lax.dynamic_index_in_dim(
        mask_rows.reshape(rows_dev, cols_dev, n_col), q, 2, keepdims=False
    ).astype(jnp.float32)
    place = jnp.stack([p, q, jnp.int32(n_row), jnp.int32(n_col)])
    x = front.reshape(rows_dev * blk * cols_dev, blk)
    values = rhs.reshape(count, rows_dev, blk)

    top = front[0, 0, :, :, 0, :] * pattern[0][None, :, None]
    shape = top.shape
    a_id = lax.broadcasted_iota(jnp.int32, shape, 0)
    m_id = lax.broadcasted_iota(jnp.int32, shape, 1)
    b_id = lax.broadcasted_iota(jnp.int32, shape, 2)
    at_diag = (a_id == b_id) & (m_id * n_col + q == p)
    top = top + jnp.where(at_diag, support[0, 0][None, None, :], 0.0)
    sent = jnp.concatenate(
        [top.reshape(n_row, sub * cols_dev, blk), values[:, 0, :].reshape(n_row, -1, blk)], axis=1
    )
    got = lax.all_to_all(sent, "row", 0, 0)[:KB]
    mine = got[:, : sub * cols_dev].reshape(KB, sub, cols_dev, blk).transpose(1, 0, 2, 3)
    mine = mine.reshape(sub * KB * cols_dev, blk)
    mine_rhs = got[:, sub * cols_dev :].reshape(KB, blk)

    def to_all(part):
        sent = jnp.broadcast_to(part[None], (n_row,) + part.shape)
        return lax.all_to_all(sent, "row", 0, 0).reshape(-1, blk)

    cols_got = lax.all_gather(mine, "row").reshape(-1, blk)
    every = lax.all_gather(mine, "col").reshape(n_col, sub, KB, rows_dev, halves, blk)
    diag_part = every[:KB, :, :, 0, 0].transpose(1, 2, 0, 3).reshape(sub, KB * KB, blk)
    rhs_part = jnp.concatenate([mine_rhs, jnp.zeros((sub - KB, blk), jnp.float32)], axis=0)
    diag_part = jnp.concatenate([diag_part, rhs_part[:, None, :]], axis=1)
    diag_got = to_all(diag_part.reshape(-1, blk))
    to_rows = every.transpose(4, 0, 1, 2, 3, 5).reshape(n_row, sub * KB * rows_dev, blk)
    rows_got = lax.all_to_all(to_rows, "row", 0, 0).reshape(-1, blk)

    inv, found = factor_call(diag_got, count)
    factor, solved = finish_call(
        place, pattern.reshape(-1), x, support[:, 0, :], values.reshape(-1, blk), rows_got,
        cols_got, inv, found,
    )
    return (factor.reshape(front.shape), solved.reshape(rhs.shape))


def solution(mesh):
    placed = (
        P(None, "row", None, None, "col", None),
        P(None, "row", None),
        P(),
        P("col", None, "row", None),
    )
    return jax.shard_map(
        shards,
        mesh=mesh,
        in_specs=placed,
        out_specs=(P(None, "row", None, None, "col", None), P("col", None, "row", None)),
        check_vma=False,
    )
```

```python
import jax
import jax.numpy as jnp
from jax import lax
from jax.experimental import pallas as pl
from jax.experimental.pallas import tpu as pltpu
from jax.sharding import PartitionSpec as P

KB = 3
SPAN = 32
STEP = 8

precise = lax.Precision.HIGHEST


def tdot(a, b):
    return lax.dot_general(
        a, b, (((0,), (0,)), ((), ())), precision=precise, preferred_element_type=jnp.float32
    )


def ndot(a, b):
    return jnp.dot(a, b, precision=precise, preferred_element_type=jnp.float32)


def rdot(a, b):
    return lax.dot_general(
        a, b, (((1,), (1,)), ((), ())), precision=precise, preferred_element_type=jnp.float32
    )


def spread(x, row):
    return jnp.broadcast_to(x[row : row + 1, :], x.shape)


def eliminate_diagonal(aug_ref):
    blk = aug_ref.shape[0]
    sub = lax.broadcasted_iota(jnp.int32, (STEP, blk), 0)
    parts = SPAN // STEP
    for g in range(blk // SPAN):
        base = g * SPAN
        rows = [slice(base + STEP * j, base + STEP * (j + 1)) for j in range(parts)]
        left = [aug_ref[rows[j], :blk] for j in range(parts)]
        right = [aug_ref[rows[j], blk:] for j in range(parts)]
        for i in range(parts):
            c0 = base + STEP * i
            cols = [
                jnp.broadcast_to(left[i][:, c0 + u : c0 + u + 1], (STEP, blk)) for u in range(STEP)
            ]
            pivots = jnp.ones((STEP, blk), jnp.float32)
            inv = []
            tops = {}
            for t in range(STEP):
                pivot = spread(cols[t], t)
                pivots = jnp.where(sub == t, pivot, pivots)
                inv.append(1.0 / pivot)
                ratio = jnp.where(sub > t, cols[t] * inv[t], 0.0)
                for u in range(t + 1, STEP):
                    tops[t, u] = spread(cols[u], t)
                    cols[u] = cols[u] - ratio * tops[t, u]
                left[i] = left[i] - ratio * spread(left[i], t)
                right[i] = right[i] - ratio * spread(right[i], t)
            for j in range(i + 1, parts):
                below = [
                    jnp.broadcast_to(left[j][:, c0 + u : c0 + u + 1], (STEP, blk))
                    for u in range(STEP)
                ]
                for t in range(STEP):
                    ratio = below[t] * inv[t]
                    for u in range(t + 1, STEP):
                        below[u] = below[u] - ratio * tops[t, u]
                    left[j] = left[j] - ratio * spread(left[i], t)
                    right[j] = right[j] - ratio * spread(right[i], t)
            scale = lax.rsqrt(pivots)
            left[i] = left[i] * scale
            right[i] = right[i] * scale
        for j in range(parts):
            aug_ref[rows[j], :blk] = left[j]
            aug_ref[rows[j], blk:] = right[j]
        end = base + SPAN
        if end < blk:
            done = aug_ref[base:end, :]
            term = tdot(done[:, :blk], done)
            aug_ref[end:, :] = aug_ref[end:, :] - term[end:, :]


def factor_kernel(diag_ref, inv_hbm, found_ref, inv_ref, a_ref, aug_ref, sem):
    blk = aug_ref.shape[0]
    size = inv_ref.shape[0]
    count = found_ref.shape[0]
    pitch = KB * KB + 1
    for k in range(KB):
        for j in range(k, KB):
            a_ref[k * blk : (k + 1) * blk, j * blk : (j + 1) * blk] = diag_ref[
                pl.ds(k * KB + j, blk, stride=pitch), :
            ]
    inv_ref[...] = jnp.zeros(inv_ref.shape, jnp.float32)
    eye = lax.broadcasted_iota(jnp.int32, (blk, blk), 0) == lax.broadcasted_iota(
        jnp.int32, (blk, blk), 1
    )
    stores = []
    for k in range(KB):
        k0, k1 = k * blk, (k + 1) * blk
        aug_ref[:, :blk] = a_ref[k0:k1, k0:k1]
        aug_ref[:, blk:] = eye.astype(jnp.float32)
        eliminate_diagonal(aug_ref)
        own = aug_ref[:, blk:]
        if k > 0:
            inv_ref[k0:k1, :k0] = ndot(own, inv_ref[k0:k1, :k0])
        inv_ref[k0:k1, k0:k1] = own
        store = pltpu.make_async_copy(inv_ref.at[k0:k1, :], inv_hbm.at[k0:k1, :], sem.at[k])
        store.start()
        stores.append(store)
        if k1 < size:
            up = ndot(own, a_ref[k0:k1, k1:])
            a_ref[k1:, k1:] = a_ref[k1:, k1:] - tdot(up, up)
            inv_ref[k1:, :k1] = inv_ref[k1:, :k1] - tdot(up, inv_ref[k0:k1, :k1])
    first = jnp.concatenate(
        [
            diag_ref[pl.ds(k * pitch + pitch - 1, count, stride=diag_ref.shape[0] // count), :]
            for k in range(KB)
        ],
        axis=1,
    )
    found_ref[...] = rdot(first, inv_ref[...])
    for store in stores:
        store.wait()


def gather(got_ref, wide, to_ref):
    blk = got_ref.shape[1]
    for k in range(KB):
        for j in range(wide):
            to_ref[k * blk : (k + 1) * blk, j * blk : (j + 1) * blk] = got_ref[
                pl.ds(k * wide + j, blk, stride=KB * wide), :
            ]


def solve(inv_ref, to_ref, blk):
    for k in reversed(range(KB)):
        k0, k1 = k * blk, (k + 1) * blk
        to_ref[k0:k1, :] = ndot(inv_ref[k0:k1, :k1], to_ref[:k1, :])


def finish_kernel(
    where_ref, pattern_ref, x_hbm, cols_hbm, inv_hbm, rhs_hbm, support_ref, rows_ref, found_ref,
    out_hbm, solved_ref, x_ref, cols_ref, inv_ref, rhs_ref, out_ref, row_ref, col_ref, sems,
    out_sem,
):
    p = where_ref[0]
    q = where_ref[1]
    n_row = where_ref[2]
    n_col = where_ref[3]
    rows_dev, blk = support_ref.shape
    wide = col_ref.shape[1] // blk
    count = found_ref.shape[0]
    part = blk * wide
    loads = [
        pltpu.make_async_copy(src, dst, sems.at[i])
        for i, (src, dst) in enumerate(
            ((inv_hbm, inv_ref), (cols_hbm, cols_ref), (x_hbm, x_ref), (rhs_hbm, rhs_ref))
        )
    ]
    for load in loads:
        load.start()
    gather(rows_ref, rows_dev, row_ref)
    loads[0].wait()
    solve(inv_ref, row_ref, blk)
    loads[3].wait()
    rest = ndot(found_ref[...], row_ref[...])
    for l in range(rows_dev):
        got = rhs_ref[pl.ds(l, count, stride=rows_dev), :] - rest[:, l * blk : (l + 1) * blk]
        if l == 0:
            for k in range(KB):
                got = jnp.where(p == k, found_ref[:, k * blk : (k + 1) * blk], got)
        solved_ref[pl.ds(l, count, stride=rows_dev), :] = got

    loads[1].wait()
    gather(cols_ref, wide, col_ref)
    solve(inv_ref, col_ref, blk)
    ri = lax.broadcasted_iota(jnp.int32, (blk, blk), 0)
    ci = lax.broadcasted_iota(jnp.int32, (blk, blk), 1)
    loads[2].wait()
    stores = []
    pair = 2
    for g in range(rows_dev // pair):
        term = tdot(row_ref[:, g * pair * blk : (g + 1) * pair * blk], col_ref[...])
        for h in range(pair):
            l = g * pair + h
            mine = row_ref[:, l * blk : (l + 1) * blk]
            row_id = l * n_row + p
            diag = jnp.where(
                ri == ci, jnp.broadcast_to(support_ref[l : l + 1, :], (blk, blk)), 0.0
            )
            for m in range(wide):
                col_id = m * n_col + q
                got = x_ref[pl.ds(l * part + m, blk, stride=wide), :]
                got = got * pattern_ref[l * wide + m]
                got = got - term[h * blk : (h + 1) * blk, m * blk : (m + 1) * blk]
                got = got + jnp.where(row_id == col_id, diag, 0.0)
                if m == 0:
                    piece = mine[:blk, :]
                    for k in range(1, KB):
                        piece = jnp.where(q == k, mine[k * blk : (k + 1) * blk, :], piece)
                    piece = piece.T
                    if l == 0:
                        piece = jnp.where((row_id == col_id) & (ri < ci), 0.0, piece)
                    got = jnp.where(q < KB, piece, got)
                if l == 0:
                    got = jnp.where((row_id < KB) & (col_id > row_id), 0.0, got)
                out_ref[pl.ds(l * part + m, blk, stride=wide), :] = got
        span = pl.ds(g * pair * part, pair * part)
        store = pltpu.make_async_copy(out_ref.at[span, :], out_hbm.at[span, :], out_sem.at[g])
        store.start()
        stores.append(store)
    for store in stores:
        store.wait()


def factor_call(diag, count):
    blk = diag.shape[1]
    size = KB * blk
    return pl.pallas_call(
        factor_kernel,
        out_shape=(
            jax.ShapeDtypeStruct((size, size), jnp.float32),
            jax.ShapeDtypeStruct((count, size), jnp.float32),
        ),
        out_specs=(pl.BlockSpec(memory_space=pltpu.HBM), pl.BlockSpec(memory_space=pltpu.VMEM)),
        scratch_shapes=[
            pltpu.VMEM((size, size), jnp.float32),
            pltpu.VMEM((size, size), jnp.float32),
            pltpu.VMEM((blk, 2 * blk), jnp.float32),
            pltpu.SemaphoreType.DMA((KB,)),
        ],
        compiler_params=pltpu.CompilerParams(vmem_limit_bytes=4 << 20),
        name="factor",
    )(diag)


def finish_call(place, pattern, x, support, rhs, rows, cols, inv, found):
    rows_dev, blk = support.shape
    size = inv.shape[0]
    wide = x.shape[0] // (rows_dev * blk)
    scalars = pl.BlockSpec(memory_space=pltpu.SMEM)
    far = pl.BlockSpec(memory_space=pltpu.HBM)
    near = pl.BlockSpec(memory_space=pltpu.VMEM)
    return pl.pallas_call(
        finish_kernel,
        in_specs=[scalars, scalars, far, far, far, far] + [near] * 3,
        out_specs=(far, near),
        out_shape=(
            jax.ShapeDtypeStruct(x.shape, jnp.float32),
            jax.ShapeDtypeStruct(rhs.shape, jnp.float32),
        ),
        scratch_shapes=[
            pltpu.VMEM(x.shape, jnp.float32),
            pltpu.VMEM(cols.shape, jnp.float32),
            pltpu.VMEM(inv.shape, jnp.float32),
            pltpu.VMEM(rhs.shape, jnp.float32),
            pltpu.VMEM(x.shape, jnp.float32),
            pltpu.VMEM((size, rows_dev * blk), jnp.float32),
            pltpu.VMEM((size, wide * blk), jnp.float32),
            pltpu.SemaphoreType.DMA((4,)),
            pltpu.SemaphoreType.DMA((rows_dev // 2,)),
        ],
        compiler_params=pltpu.CompilerParams(vmem_limit_bytes=14 << 20),
        name="finish",
    )(
        place,
        pattern,
        x,
        cols,
        pltpu.with_memory_space_constraint(inv, pltpu.HBM),
        rhs,
        support,
        rows,
        found,
    )


def start_kernel(where_ref, x_hbm, rhs_hbm, mask_ref, support_ref, out_ref, x_ref, rhs_ref, sems):
    p = where_ref[0]
    q = where_ref[1]
    n_col = where_ref[3]
    blk = support_ref.shape[1]
    n_row, pitch = out_ref.shape[0], out_ref.shape[1]
    wide = x_ref.shape[0] // blk
    sub = blk // n_row
    loads = [
        pltpu.make_async_copy(x_hbm.at[pl.ds(0, blk * wide), :], x_ref, sems.at[0]),
        pltpu.make_async_copy(rhs_hbm, rhs_ref, sems.at[1]),
    ]
    for load in loads:
        load.start()
    lane = lax.broadcasted_iota(jnp.int32, (wide, blk), 1)
    col_id = lax.broadcasted_iota(jnp.int32, (wide, blk), 0) * n_col + q
    own = jnp.broadcast_to(mask_ref[pl.ds(p, 1), :], (wide, blk)).astype(jnp.float32)
    keep = jnp.sum(jnp.where(lane == col_id, own, 0.0), axis=1, keepdims=True)
    keep = jnp.broadcast_to(keep, (wide, blk))
    added = jnp.where(col_id == p, jnp.broadcast_to(support_ref[0:1, :], (wide, blk)), 0.0)
    loads[1].wait()
    step = rhs_ref.shape[0] // n_row
    first = rhs_ref[pl.ds(0, n_row, stride=step), :]
    zero = jnp.zeros((pitch - sub * wide - 1, blk), jnp.float32)
    loads[0].wait()
    for r in range(n_row):
        for s in range(sub):
            a = r * sub + s
            got = x_ref[a * wide : (a + 1) * wide, :] * keep + jnp.where(lane == a, added, 0.0)
            out_ref[r, s * wide : (s + 1) * wide, :] = got
        out_ref[r, sub * wide :, :] = jnp.concatenate([first[r : r + 1, :], zero], axis=0)


def start_call(place, x, rhs, mask, support, n_row, wide):
    blk = support.shape[1]
    far = pl.BlockSpec(memory_space=pltpu.HBM)
    near = pl.BlockSpec(memory_space=pltpu.VMEM)
    pitch = blk // n_row * wide + 8
    return pl.pallas_call(
        start_kernel,
        in_specs=[pl.BlockSpec(memory_space=pltpu.SMEM), far, far, near, near],
        out_specs=near,
        out_shape=jax.ShapeDtypeStruct((n_row, pitch, blk), jnp.float32),
        scratch_shapes=[
            pltpu.VMEM((blk * wide, blk), jnp.float32),
            pltpu.VMEM(rhs.shape, jnp.float32),
            pltpu.SemaphoreType.DMA((2,)),
        ],
        compiler_params=pltpu.CompilerParams(vmem_limit_bytes=4 << 20),
        name="start",
    )(place, x, rhs, mask, support)


def shards(front, support, mask, rhs):
    n_row = lax.axis_size("row")
    n_col = lax.axis_size("col")
    p = lax.axis_index("row")
    q = lax.axis_index("col")
    rows_dev = front.shape[0]
    blk = front.shape[2]
    cols_dev = front.shape[3]
    halves = n_row // n_col
    sub = blk // n_row
    count = rhs.shape[0]
    mask_rows = lax.dynamic_index_in_dim(mask.reshape(rows_dev, n_row, -1), p, 1, keepdims=False)
    pattern = lax.dynamic_index_in_dim(
        mask_rows.reshape(rows_dev, cols_dev, n_col), q, 2, keepdims=False
    ).astype(jnp.float32)
    place = jnp.stack([p, q, jnp.int32(n_row), jnp.int32(n_col)])
    x = pltpu.with_memory_space_constraint(
        front.reshape(rows_dev * blk * cols_dev, blk), pltpu.HBM
    )
    values = pltpu.with_memory_space_constraint(rhs.reshape(count * rows_dev, blk), pltpu.HBM)

    sent = start_call(place, x, values, mask, support[:, 0, :], n_row, cols_dev)
    got = lax.all_to_all(sent, "row", 0, 0)[:KB]
    mine = got[:, : sub * cols_dev].reshape(KB, sub, cols_dev, blk).transpose(1, 0, 2, 3)
    mine = mine.reshape(sub * KB * cols_dev, blk)
    mine_rhs = got[:, sub * cols_dev]

    def to_all(part):
        sent = jnp.broadcast_to(part[None], (n_row,) + part.shape)
        return lax.all_to_all(sent, "row", 0, 0).reshape(-1, blk)

    cols_got = to_all(mine)
    every = lax.all_gather(mine, "col").reshape(n_col, sub, KB, rows_dev, halves, blk)
    diag_part = every[:KB, :, :, 0, 0].transpose(1, 2, 0, 3).reshape(sub, KB * KB, blk)
    rhs_part = jnp.concatenate([mine_rhs, jnp.zeros((sub - KB, blk), jnp.float32)], axis=0)
    diag_part = jnp.concatenate([diag_part, rhs_part[:, None, :]], axis=1)
    diag_part, cols_got = lax.optimization_barrier((diag_part, cols_got))
    diag_got = to_all(diag_part.reshape(-1, blk))
    to_rows = every.transpose(4, 0, 1, 2, 3, 5).reshape(n_row, sub * KB * rows_dev, blk)
    rows_got = lax.all_to_all(to_rows, "row", 0, 0).reshape(-1, blk)

    inv, found = factor_call(diag_got, count)
    factor, solved = finish_call(
        place, pattern.reshape(-1), x, support[:, 0, :], values, rows_got,
        cols_got, inv, found,
    )
    return (factor.reshape(front.shape), solved.reshape(rhs.shape))


def solution(mesh):
    placed = (
        P(None, "row", None, None, "col", None),
        P(None, "row", None),
        P(),
        P("col", None, "row", None),
    )
    return jax.shard_map(
        shards,
        mesh=mesh,
        in_specs=placed,
        out_specs=(P(None, "row", None, None, "col", None), P("col", None, "row", None)),
        check_vma=False,
    )
```

```python
import functools

import jax
import jax.numpy as jnp
from jax import lax
from jax.experimental import pallas as pl
from jax.experimental.pallas import tpu as pltpu
from jax.sharding import PartitionSpec as P

KB = 3
SPAN = 64
STEP = 8
UPPER = KB * (KB + 1) // 2

precise = lax.Precision.HIGHEST


def tdot(a, b):
    return lax.dot_general(
        a, b, (((0,), (0,)), ((), ())), precision=precise, preferred_element_type=jnp.float32
    )


def ndot(a, b):
    return jnp.dot(a, b, precision=precise, preferred_element_type=jnp.float32)


def rdot(a, b):
    return lax.dot_general(
        a, b, (((1,), (1,)), ((), ())), precision=precise, preferred_element_type=jnp.float32
    )


def spread(x, row):
    return jnp.broadcast_to(x[row : row + 1, :], x.shape)


def eliminate_diagonal(aug_ref):
    blk = aug_ref.shape[0]
    sub = lax.broadcasted_iota(jnp.int32, (STEP, blk), 0)
    parts = SPAN // STEP
    for g in range(blk // SPAN):
        base = g * SPAN
        rows = [slice(base + STEP * j, base + STEP * (j + 1)) for j in range(parts)]
        left = [aug_ref[rows[j], :blk] for j in range(parts)]
        right = [aug_ref[rows[j], blk:] for j in range(parts)]
        for i in range(parts):
            c0 = base + STEP * i

            def columns(j):
                return [
                    jnp.broadcast_to(left[j][:, c0 + u : c0 + u + 1], (STEP, blk))
                    for u in range(STEP)
                ]

            cols = columns(i)
            pivots = jnp.ones((STEP, blk), jnp.float32)
            pairs = []
            for t in range(0, STEP, 2):
                a, b = spread(cols[t], t), spread(cols[t], t + 1)
                c = spread(cols[t + 1], t + 1)
                det = a * c - b * b
                rdet = 1.0 / det
                ra = 1.0 / a
                pivots = jnp.where(sub == t, a, jnp.where(sub == t + 1, det * ra, pivots))
                below = sub > t + 1
                m0 = jnp.where(below, (c * cols[t] - b * cols[t + 1]) * rdet, 0.0)
                m1 = jnp.where(below, (a * cols[t + 1] - b * cols[t]) * rdet, 0.0)
                tops = {}
                for u in range(t + 2, STEP):
                    tops[u] = spread(cols[u], t), spread(cols[u], t + 1)
                    cols[u] = cols[u] - (m0 * tops[u][0] + m1 * tops[u][1])
                lt = spread(left[i], t), spread(left[i], t + 1)
                rt = spread(right[i], t), spread(right[i], t + 1)
                m0 = jnp.where(sub == t + 1, b * ra, m0)
                left[i] = left[i] - (m0 * lt[0] + m1 * lt[1])
                right[i] = right[i] - (m0 * rt[0] + m1 * rt[1])
                pairs.append((a, b, c, rdet, tops, lt, rt))
            for j in range(i + 1, parts):
                cols = columns(j)
                for n, (a, b, c, rdet, tops, lt, rt) in enumerate(pairs):
                    t = 2 * n
                    m0 = (c * cols[t] - b * cols[t + 1]) * rdet
                    m1 = (a * cols[t + 1] - b * cols[t]) * rdet
                    for u in range(t + 2, STEP):
                        cols[u] = cols[u] - (m0 * tops[u][0] + m1 * tops[u][1])
                    left[j] = left[j] - (m0 * lt[0] + m1 * lt[1])
                    right[j] = right[j] - (m0 * rt[0] + m1 * rt[1])
            scale = lax.rsqrt(pivots)
            left[i] = left[i] * scale
            right[i] = right[i] * scale
        for j in range(parts):
            aug_ref[rows[j], :blk] = left[j]
            aug_ref[rows[j], blk:] = right[j]
        end = base + SPAN
        if end < blk:
            done = aug_ref[base:end, :]
            term = tdot(done[:, :blk], done)
            aug_ref[end:, :] = aug_ref[end:, :] - term[end:, :]


def factor_kernel(diag_ref, inv_hbm, found_ref, inv_ref, a_ref, aug_ref, sem):
    blk = aug_ref.shape[0]
    size = inv_ref.shape[0]
    count = found_ref.shape[0]
    pitch = UPPER + 2
    t = 0
    for k in range(KB):
        for j in range(k, KB):
            a_ref[k * blk : (k + 1) * blk, j * blk : (j + 1) * blk] = diag_ref[
                pl.ds(t, blk, stride=pitch), :
            ]
            t += 1
    inv_ref[...] = jnp.zeros(inv_ref.shape, jnp.float32)
    eye = lax.broadcasted_iota(jnp.int32, (blk, blk), 0) == lax.broadcasted_iota(
        jnp.int32, (blk, blk), 1
    )
    stores = []
    for k in range(KB):
        k0, k1 = k * blk, (k + 1) * blk
        aug_ref[:, :blk] = a_ref[k0:k1, k0:k1]
        aug_ref[:, blk:] = eye.astype(jnp.float32)
        eliminate_diagonal(aug_ref)
        own = aug_ref[:, blk:]
        if k > 0:
            inv_ref[k0:k1, :k0] = ndot(own, inv_ref[k0:k1, :k0])
        inv_ref[k0:k1, k0:k1] = own
        store = pltpu.make_async_copy(inv_ref.at[k0:k1, :], inv_hbm.at[k0:k1, :], sem.at[k])
        store.start()
        stores.append(store)
        if k1 < size:
            up = ndot(own, a_ref[k0:k1, k1:])
            a_ref[k1:, k1:] = a_ref[k1:, k1:] - tdot(up, up)
            inv_ref[k1:, :k1] = inv_ref[k1:, :k1] - tdot(up, inv_ref[k0:k1, :k1])
    first = jnp.concatenate(
        [
            diag_ref[pl.ds(k * pitch + UPPER, count, stride=diag_ref.shape[0] // count), :]
            for k in range(KB)
        ],
        axis=1,
    )
    found_ref[...] = rdot(first, inv_ref[...])
    for store in stores:
        store.wait()


def gather(got_ref, wide, to_ref):
    blk = got_ref.shape[1]
    for k in range(KB):
        for j in range(wide):
            to_ref[k * blk : (k + 1) * blk, j * blk : (j + 1) * blk] = got_ref[
                pl.ds(k * wide + j, blk, stride=KB * wide), :
            ]


def solve(inv_ref, to_ref, blk):
    for k in reversed(range(KB)):
        k0, k1 = k * blk, (k + 1) * blk
        to_ref[k0:k1, :] = ndot(inv_ref[k0:k1, :k1], to_ref[:k1, :])


def finish_kernel(
    where_ref, x_hbm, cols_hbm, inv_hbm, rhs_hbm, mask_hbm, support_hbm, rows_ref, found_ref,
    out_hbm, solved_ref, x_ref, cols_ref, inv_ref, rhs_ref, mask_ref, support_ref, out_ref,
    row_ref, col_ref, sems, out_sem,
):
    p = where_ref[0]
    q = where_ref[1]
    n_row = where_ref[2]
    n_col = where_ref[3]
    rows_dev, blk = support_ref.shape
    wide = col_ref.shape[1] // blk
    count = found_ref.shape[0]
    part = blk * wide
    loads = [
        pltpu.make_async_copy(src, dst, sems.at[i])
        for i, (src, dst) in enumerate(
            ((inv_hbm, inv_ref), (cols_hbm, cols_ref), (x_hbm, x_ref), (rhs_hbm, rhs_ref),
             (mask_hbm, mask_ref), (support_hbm, support_ref))
        )
    ]
    for load in loads:
        load.start()
    gather(rows_ref, rows_dev, row_ref)
    loads[0].wait()
    solve(inv_ref, row_ref, blk)
    loads[3].wait()
    rest = ndot(found_ref[...], row_ref[...])
    for l in range(rows_dev):
        got = rhs_ref[pl.ds(l, count, stride=rows_dev), :] - rest[:, l * blk : (l + 1) * blk]
        if l == 0:
            for k in range(KB):
                got = jnp.where(p == k, found_ref[:, k * blk : (k + 1) * blk], got)
        solved_ref[pl.ds(l, count, stride=rows_dev), :] = got

    loads[1].wait()
    gather(cols_ref, wide, col_ref)
    solve(inv_ref, col_ref, blk)
    ri = lax.broadcasted_iota(jnp.int32, (blk, blk), 0)
    ci = lax.broadcasted_iota(jnp.int32, (blk, blk), 1)
    loads[4].wait()
    loads[5].wait()
    loads[2].wait()
    stores = []
    pair = 2
    for g in range(rows_dev // pair):
        term = tdot(row_ref[:, g * pair * blk : (g + 1) * pair * blk], col_ref[...])
        for h in range(pair):
            l = g * pair + h
            mine = row_ref[:, l * blk : (l + 1) * blk]
            row_id = l * n_row + p
            keep = kept(mask_ref, row_id, q, n_col, wide)
            diag = jnp.where(
                ri == ci, jnp.broadcast_to(support_ref[l : l + 1, :], (blk, blk)), 0.0
            )
            for m in range(wide):
                col_id = m * n_col + q
                got = x_ref[pl.ds(l * part + m, blk, stride=wide), :]
                got = got * jnp.broadcast_to(keep[m : m + 1, :], (blk, blk))
                got = got - term[h * blk : (h + 1) * blk, m * blk : (m + 1) * blk]
                got = got + jnp.where(row_id == col_id, diag, 0.0)
                if m == 0:
                    piece = mine[:blk, :]
                    for k in range(1, KB):
                        piece = jnp.where(q == k, mine[k * blk : (k + 1) * blk, :], piece)
                    piece = piece.T
                    if l == 0:
                        piece = jnp.where((row_id == col_id) & (ri < ci), 0.0, piece)
                    got = jnp.where(q < KB, piece, got)
                if l == 0:
                    got = jnp.where((row_id < KB) & (col_id > row_id), 0.0, got)
                out_ref[pl.ds(l * part + m, blk, stride=wide), :] = got
        span = pl.ds(g * pair * part, pair * part)
        store = pltpu.make_async_copy(out_ref.at[span, :], out_hbm.at[span, :], out_sem.at[g])
        store.start()
        stores.append(store)
    for store in stores:
        store.wait()


def factor_call(diag, count):
    blk = diag.shape[1]
    size = KB * blk
    return pl.pallas_call(
        factor_kernel,
        out_shape=(
            jax.ShapeDtypeStruct((size, size), jnp.float32),
            jax.ShapeDtypeStruct((count, size), jnp.float32),
        ),
        out_specs=(pl.BlockSpec(memory_space=pltpu.HBM), pl.BlockSpec(memory_space=pltpu.VMEM)),
        scratch_shapes=[
            pltpu.VMEM((size, size), jnp.float32),
            pltpu.VMEM((size, size), jnp.float32),
            pltpu.VMEM((blk, 2 * blk), jnp.float32),
            pltpu.SemaphoreType.DMA((KB,)),
        ],
        compiler_params=pltpu.CompilerParams(vmem_limit_bytes=4 << 20),
        name="factor",
    )(diag)


def finish_call(place, x, mask, support, rhs, rows, cols, inv, found):
    rows_dev, blk = support.shape
    size = inv.shape[0]
    wide = x.shape[0] // (rows_dev * blk)
    scalars = pl.BlockSpec(memory_space=pltpu.SMEM)
    far = pl.BlockSpec(memory_space=pltpu.HBM)
    near = pl.BlockSpec(memory_space=pltpu.VMEM)
    return pl.pallas_call(
        finish_kernel,
        in_specs=[scalars] + [far] * 6 + [near] * 2,
        out_specs=(far, near),
        out_shape=(
            jax.ShapeDtypeStruct(x.shape, jnp.float32),
            jax.ShapeDtypeStruct(rhs.shape, jnp.float32),
        ),
        scratch_shapes=[
            pltpu.VMEM(x.shape, jnp.float32),
            pltpu.VMEM(cols.shape, jnp.float32),
            pltpu.VMEM(inv.shape, jnp.float32),
            pltpu.VMEM(rhs.shape, jnp.float32),
            pltpu.VMEM(mask.shape, jnp.int32),
            pltpu.VMEM(support.shape, jnp.float32),
            pltpu.VMEM(x.shape, jnp.float32),
            pltpu.VMEM((size, rows_dev * blk), jnp.float32),
            pltpu.VMEM((size, wide * blk), jnp.float32),
            pltpu.SemaphoreType.DMA((6,)),
            pltpu.SemaphoreType.DMA((rows_dev // 2,)),
        ],
        compiler_params=pltpu.CompilerParams(vmem_limit_bytes=14 << 20),
        name="finish",
    )(
        place,
        x,
        cols,
        pltpu.with_memory_space_constraint(inv, pltpu.HBM),
        rhs,
        mask,
        support,
        rows,
        found,
    )


def kept(mask_ref, row_id, q, n_col, wide):
    blk = mask_ref.shape[1]
    lane = lax.broadcasted_iota(jnp.int32, (wide, blk), 1)
    col_id = lax.broadcasted_iota(jnp.int32, (wide, blk), 0) * n_col + q
    own = jnp.broadcast_to(mask_ref[pl.ds(row_id, 1), :], (wide, blk)).astype(jnp.float32)
    keep = jnp.sum(jnp.where(lane == col_id, own, 0.0), axis=1, keepdims=True)
    return jnp.broadcast_to(keep, (wide, blk))


def start_kernel(
    where_ref, x_hbm, rhs_hbm, mask_hbm, support_hbm, out_ref, x_ref, rhs_ref, mask_ref,
    support_ref, sems,
):
    p = where_ref[0]
    q = where_ref[1]
    n_col = where_ref[3]
    blk = support_ref.shape[1]
    n_row, pitch = out_ref.shape[0], out_ref.shape[1]
    wide = x_ref.shape[0] // blk
    sub = blk // n_row
    pairs = (
        (mask_hbm, mask_ref), (support_hbm, support_ref), (rhs_hbm, rhs_ref),
        (x_hbm.at[pl.ds(0, blk * wide), :], x_ref),
    )
    loads = [pltpu.make_async_copy(src, dst, sems.at[i]) for i, (src, dst) in enumerate(pairs)]
    for load in loads:
        load.start()
    for load in loads[:3]:
        load.wait()
    lane = lax.broadcasted_iota(jnp.int32, (wide, blk), 1)
    col_id = lax.broadcasted_iota(jnp.int32, (wide, blk), 0) * n_col + q
    keep = kept(mask_ref, p, q, n_col, wide)
    added = jnp.where(col_id == p, jnp.broadcast_to(support_ref[0:1, :], (wide, blk)), 0.0)
    step = rhs_ref.shape[0] // n_row
    first = rhs_ref[pl.ds(0, n_row, stride=step), :]
    zero = jnp.zeros((pitch - sub * wide - 1, blk), jnp.float32)
    loads[3].wait()
    for r in range(n_row):
        for s in range(sub):
            a = r * sub + s
            got = x_ref[a * wide : (a + 1) * wide, :] * keep + jnp.where(lane == a, added, 0.0)
            out_ref[r, s * wide : (s + 1) * wide, :] = got
        out_ref[r, sub * wide :, :] = jnp.concatenate([first[r : r + 1, :], zero], axis=0)


def start_call(place, x, rhs, mask, support, n_row, wide):
    blk = support.shape[1]
    far = pl.BlockSpec(memory_space=pltpu.HBM)
    pitch = blk // n_row * wide + 8
    return pl.pallas_call(
        start_kernel,
        in_specs=[pl.BlockSpec(memory_space=pltpu.SMEM), far, far, far, far],
        out_specs=pl.BlockSpec(memory_space=pltpu.VMEM),
        out_shape=jax.ShapeDtypeStruct((n_row, pitch, blk), jnp.float32),
        scratch_shapes=[
            pltpu.VMEM((blk * wide, blk), jnp.float32),
            pltpu.VMEM(rhs.shape, jnp.float32),
            pltpu.VMEM(mask.shape, jnp.int32),
            pltpu.VMEM(support.shape, jnp.float32),
            pltpu.SemaphoreType.DMA((4,)),
        ],
        compiler_params=pltpu.CompilerParams(vmem_limit_bytes=4 << 20),
        name="start",
    )(place, x, rhs, mask, support)


def send_copies(src_ref, out_hbm, sems):
    copies = [
        pltpu.make_async_copy(src_ref, out_hbm.at[r], sems.at[r]) for r in range(out_hbm.shape[0])
    ]
    for copy in copies:
        copy.start()
    for copy in copies:
        copy.wait()


def slice_kernel(got_hbm, mine_ref, out_hbm, got_ref, sem, sems, *, pitch, sub, wide):
    load = pltpu.make_async_copy(got_hbm.at[pl.ds(0, KB * pitch), :], got_ref, sem)
    load.start()
    load.wait()
    for a in range(sub):
        for k in range(KB):
            at = (a * KB + k) * wide
            mine_ref[at : at + wide, :] = got_ref[k * pitch + a * wide : k * pitch + (a + 1) * wide, :]
    send_copies(mine_ref, out_hbm, sems)


def slice_call(got, n_row, sub, wide):
    blk = got.shape[-1]
    rows = sub * KB * wide
    near = pl.BlockSpec(memory_space=pltpu.VMEM)
    return pl.pallas_call(
        functools.partial(slice_kernel, pitch=got.shape[1], sub=sub, wide=wide),
        in_specs=[pl.BlockSpec(memory_space=pltpu.HBM)],
        out_specs=(near, pl.BlockSpec(memory_space=pltpu.HBM)),
        out_shape=(
            jax.ShapeDtypeStruct((rows, blk), jnp.float32),
            jax.ShapeDtypeStruct((n_row, rows, blk), jnp.float32),
        ),
        scratch_shapes=[
            pltpu.VMEM((KB * got.shape[1], blk), jnp.float32),
            pltpu.SemaphoreType.DMA,
            pltpu.SemaphoreType.DMA((n_row,)),
        ],
        name="slice",
    )(got.reshape(-1, blk))


def diag_kernel(
    every_hbm, got_hbm, out_hbm, every_ref, got_ref, tile_ref, in_sems, sems, *, pitch, sub, wide
):
    rows = sub * KB * wide
    loads = [
        pltpu.make_async_copy(every_hbm.at[pl.ds(0, KB * rows), :], every_ref, in_sems.at[0]),
        pltpu.make_async_copy(got_hbm.at[pl.ds(0, KB * pitch), :], got_ref, in_sems.at[1]),
    ]
    for load in loads:
        load.start()
    for load in loads:
        load.wait()
    for a in range(sub):
        parts = []
        for k in range(KB):
            for j in range(k, KB):
                at = j * rows + (a * KB + k) * wide
                parts.append(every_ref[at : at + 1, :])
        at = min(a, KB - 1) * pitch + sub * wide
        parts.append(got_ref[at : at + 1, :])
        parts.append(jnp.zeros_like(parts[0]))
        tile_ref[a * (UPPER + 2) : (a + 1) * (UPPER + 2), :] = jnp.concatenate(parts, axis=0)
    send_copies(tile_ref, out_hbm, sems)


def diag_call(every, got, n_row, sub, wide):
    blk = got.shape[-1]
    rows = sub * (UPPER + 2)
    far = pl.BlockSpec(memory_space=pltpu.HBM)
    return pl.pallas_call(
        functools.partial(diag_kernel, pitch=got.shape[1], sub=sub, wide=wide),
        in_specs=[far, far],
        out_specs=far,
        out_shape=jax.ShapeDtypeStruct((n_row, rows, blk), jnp.float32),
        scratch_shapes=[
            pltpu.VMEM((KB * sub * KB * wide, blk), jnp.float32),
            pltpu.VMEM((KB * got.shape[1], blk), jnp.float32),
            pltpu.VMEM((rows, blk), jnp.float32),
            pltpu.SemaphoreType.DMA((2,)),
            pltpu.SemaphoreType.DMA((n_row,)),
        ],
        name="diagonal",
    )(every.reshape(-1, blk), got.reshape(-1, blk))


def shards(front, support, mask, rhs):
    n_row = lax.axis_size("row")
    n_col = lax.axis_size("col")
    p = lax.axis_index("row")
    q = lax.axis_index("col")
    rows_dev = front.shape[0]
    blk = front.shape[2]
    cols_dev = front.shape[3]
    halves = n_row // n_col
    sub = blk // n_row
    count = rhs.shape[0]
    place = jnp.stack([p, q, jnp.int32(n_row), jnp.int32(n_col)])
    x = pltpu.with_memory_space_constraint(
        front.reshape(rows_dev * blk * cols_dev, blk), pltpu.HBM
    )
    mask = pltpu.with_memory_space_constraint(mask, pltpu.HBM)
    support = pltpu.with_memory_space_constraint(support.reshape(rows_dev, blk), pltpu.HBM)
    values = pltpu.with_memory_space_constraint(rhs.reshape(count * rows_dev, blk), pltpu.HBM)

    sent = start_call(place, x, values, mask, support, n_row, cols_dev)
    got = lax.all_to_all(sent, "row", 0, 0)
    mine, cols_sent = slice_call(got, n_row, sub, cols_dev)
    cols_got = lax.all_to_all(cols_sent, "row", 0, 0).reshape(-1, blk)
    every = lax.all_gather(mine, "col")
    diag_sent = diag_call(every, got, n_row, sub, cols_dev)
    diag_sent, cols_got = lax.optimization_barrier((diag_sent, cols_got))
    diag_got = lax.all_to_all(diag_sent, "row", 0, 0).reshape(-1, blk)
    every = every.reshape(n_col, sub, KB, rows_dev, halves, blk)
    to_rows = every.transpose(4, 0, 1, 2, 3, 5).reshape(n_row, sub * KB * rows_dev, blk)
    rows_got = lax.all_to_all(to_rows, "row", 0, 0).reshape(-1, blk)

    inv, found = factor_call(diag_got, count)
    factor, solved = finish_call(
        place, x, mask, support, values, rows_got, cols_got, inv, found
    )
    return (factor.reshape(front.shape), solved.reshape(rhs.shape))


def solution(mesh):
    placed = (
        P(None, "row", None, None, "col", None),
        P(None, "row", None),
        P(),
        P("col", None, "row", None),
    )
    return jax.shard_map(
        shards,
        mesh=mesh,
        in_specs=placed,
        out_specs=(P(None, "row", None, None, "col", None), P("col", None, "row", None)),
        check_vma=False,
    )
```

```python
import jax
import jax.numpy as jnp
from jax import lax
from jax.experimental import pallas as pl
from jax.experimental.pallas import tpu as pltpu
from jax.sharding import PartitionSpec as P

KB = 3
SPAN = 64
STEP = 8
UPPER = KB * (KB + 1) // 2

precise = lax.Precision.HIGHEST


def tdot(a, b):
    return lax.dot_general(
        a, b, (((0,), (0,)), ((), ())), precision=precise, preferred_element_type=jnp.float32
    )


def ndot(a, b):
    return jnp.dot(a, b, precision=precise, preferred_element_type=jnp.float32)


def rdot(a, b):
    return lax.dot_general(
        a, b, (((1,), (1,)), ((), ())), precision=precise, preferred_element_type=jnp.float32
    )


def spread(x, row):
    return jnp.broadcast_to(x[row : row + 1, :], x.shape)


def eliminate_diagonal(aug_ref):
    blk = aug_ref.shape[0]
    sub = lax.broadcasted_iota(jnp.int32, (STEP, blk), 0)
    parts = SPAN // STEP
    for g in range(blk // SPAN):
        base = g * SPAN
        rows = [slice(base + STEP * j, base + STEP * (j + 1)) for j in range(parts)]
        left = [aug_ref[rows[j], :blk] for j in range(parts)]
        right = [aug_ref[rows[j], blk:] for j in range(parts)]
        for i in range(parts):
            c0 = base + STEP * i

            def columns(j):
                return [
                    jnp.broadcast_to(left[j][:, c0 + u : c0 + u + 1], (STEP, blk))
                    for u in range(STEP)
                ]

            cols = columns(i)
            pivots = jnp.ones((STEP, blk), jnp.float32)
            pairs = []
            for t in range(0, STEP, 2):
                a, b = spread(cols[t], t), spread(cols[t], t + 1)
                c = spread(cols[t + 1], t + 1)
                det = a * c - b * b
                rdet = 1.0 / det
                ra = 1.0 / a
                pivots = jnp.where(sub == t, a, jnp.where(sub == t + 1, det * ra, pivots))
                below = sub > t + 1
                m0 = jnp.where(below, (c * cols[t] - b * cols[t + 1]) * rdet, 0.0)
                m1 = jnp.where(below, (a * cols[t + 1] - b * cols[t]) * rdet, 0.0)
                tops = {}
                for u in range(t + 2, STEP):
                    tops[u] = spread(cols[u], t), spread(cols[u], t + 1)
                    cols[u] = cols[u] - (m0 * tops[u][0] + m1 * tops[u][1])
                lt = spread(left[i], t), spread(left[i], t + 1)
                rt = spread(right[i], t), spread(right[i], t + 1)
                m0 = jnp.where(sub == t + 1, b * ra, m0)
                left[i] = left[i] - (m0 * lt[0] + m1 * lt[1])
                right[i] = right[i] - (m0 * rt[0] + m1 * rt[1])
                pairs.append((a, b, c, rdet, tops, lt, rt))
            for j in range(i + 1, parts):
                cols = columns(j)
                for n, (a, b, c, rdet, tops, lt, rt) in enumerate(pairs):
                    t = 2 * n
                    m0 = (c * cols[t] - b * cols[t + 1]) * rdet
                    m1 = (a * cols[t + 1] - b * cols[t]) * rdet
                    for u in range(t + 2, STEP):
                        cols[u] = cols[u] - (m0 * tops[u][0] + m1 * tops[u][1])
                    left[j] = left[j] - (m0 * lt[0] + m1 * lt[1])
                    right[j] = right[j] - (m0 * rt[0] + m1 * rt[1])
            scale = lax.rsqrt(pivots)
            left[i] = left[i] * scale
            right[i] = right[i] * scale
        for j in range(parts):
            aug_ref[rows[j], :blk] = left[j]
            aug_ref[rows[j], blk:] = right[j]
        end = base + SPAN
        if end < blk:
            done = aug_ref[base:end, :]
            term = tdot(done[:, :blk], done)
            aug_ref[end:, :] = aug_ref[end:, :] - term[end:, :]


def factor_kernel(diag_ref, inv_hbm, found_ref, inv_ref, a_ref, aug_ref, sem):
    blk = aug_ref.shape[0]
    size = inv_ref.shape[0]
    count = found_ref.shape[0]
    pitch = UPPER + 2
    t = 0
    for k in range(KB):
        for j in range(k, KB):
            a_ref[k * blk : (k + 1) * blk, j * blk : (j + 1) * blk] = diag_ref[
                pl.ds(t, blk, stride=pitch), :
            ]
            t += 1
    inv_ref[...] = jnp.zeros(inv_ref.shape, jnp.float32)
    eye = lax.broadcasted_iota(jnp.int32, (blk, blk), 0) == lax.broadcasted_iota(
        jnp.int32, (blk, blk), 1
    )
    stores = []
    for k in range(KB):
        k0, k1 = k * blk, (k + 1) * blk
        aug_ref[:, :blk] = a_ref[k0:k1, k0:k1]
        aug_ref[:, blk:] = eye.astype(jnp.float32)
        eliminate_diagonal(aug_ref)
        own = aug_ref[:, blk:]
        if k > 0:
            inv_ref[k0:k1, :k0] = ndot(own, inv_ref[k0:k1, :k0])
        inv_ref[k0:k1, k0:k1] = own
        store = pltpu.make_async_copy(inv_ref.at[k0:k1, :], inv_hbm.at[k0:k1, :], sem.at[k])
        store.start()
        stores.append(store)
        if k1 < size:
            up = ndot(own, a_ref[k0:k1, k1:])
            a_ref[k1:, k1:] = a_ref[k1:, k1:] - tdot(up, up)
            inv_ref[k1:, :k1] = inv_ref[k1:, :k1] - tdot(up, inv_ref[k0:k1, :k1])
    first = jnp.concatenate(
        [
            diag_ref[pl.ds(k * pitch + UPPER, count, stride=diag_ref.shape[0] // count), :]
            for k in range(KB)
        ],
        axis=1,
    )
    found_ref[...] = rdot(first, inv_ref[...])
    for store in stores:
        store.wait()


def gather(got_ref, wide, to_ref):
    blk = got_ref.shape[1]
    for k in range(KB):
        for j in range(wide):
            to_ref[k * blk : (k + 1) * blk, j * blk : (j + 1) * blk] = got_ref[
                pl.ds(k * wide + j, blk, stride=KB * wide), :
            ]


def solve(inv_ref, to_ref, blk):
    for k in reversed(range(KB)):
        k0, k1 = k * blk, (k + 1) * blk
        to_ref[k0:k1, :] = ndot(inv_ref[k0:k1, :k1], to_ref[:k1, :])


def finish_kernel(
    where_ref, x_hbm, cols_hbm, inv_hbm, rhs_hbm, mask_hbm, support_hbm, rows_ref, found_ref,
    out_hbm, solved_ref, x_ref, cols_ref, inv_ref, rhs_ref, mask_ref, support_ref, out_ref,
    row_ref, col_ref, sems, out_sem,
):
    p = where_ref[0]
    q = where_ref[1]
    n_row = where_ref[2]
    n_col = where_ref[3]
    rows_dev, blk = support_ref.shape
    wide = col_ref.shape[1] // blk
    count = found_ref.shape[0]
    part = blk * wide
    loads = [
        pltpu.make_async_copy(src, dst, sems.at[i])
        for i, (src, dst) in enumerate(
            ((inv_hbm, inv_ref), (cols_hbm, cols_ref), (x_hbm, x_ref), (rhs_hbm, rhs_ref),
             (mask_hbm, mask_ref), (support_hbm, support_ref))
        )
    ]
    for load in loads:
        load.start()
    gather(rows_ref, rows_dev, row_ref)
    loads[0].wait()
    solve(inv_ref, row_ref, blk)
    loads[3].wait()
    rest = ndot(found_ref[...], row_ref[...])
    for l in range(rows_dev):
        got = rhs_ref[pl.ds(l, count, stride=rows_dev), :] - rest[:, l * blk : (l + 1) * blk]
        if l == 0:
            for k in range(KB):
                got = jnp.where(p == k, found_ref[:, k * blk : (k + 1) * blk], got)
        solved_ref[pl.ds(l, count, stride=rows_dev), :] = got

    loads[1].wait()
    gather(cols_ref, wide, col_ref)
    solve(inv_ref, col_ref, blk)
    ri = lax.broadcasted_iota(jnp.int32, (blk, blk), 0)
    ci = lax.broadcasted_iota(jnp.int32, (blk, blk), 1)
    loads[4].wait()
    loads[5].wait()
    loads[2].wait()
    stores = []
    pair = 2
    for g in range(rows_dev // pair):
        term = tdot(row_ref[:, g * pair * blk : (g + 1) * pair * blk], col_ref[...])
        for h in range(pair):
            l = g * pair + h
            mine = row_ref[:, l * blk : (l + 1) * blk]
            row_id = l * n_row + p
            keep = kept(mask_ref, row_id, q, n_col, wide)
            diag = jnp.where(
                ri == ci, jnp.broadcast_to(support_ref[l : l + 1, :], (blk, blk)), 0.0
            )
            for m in range(wide):
                col_id = m * n_col + q
                got = x_ref[pl.ds(l * part + m, blk, stride=wide), :]
                got = got * jnp.broadcast_to(keep[m : m + 1, :], (blk, blk))
                got = got - term[h * blk : (h + 1) * blk, m * blk : (m + 1) * blk]
                got = got + jnp.where(row_id == col_id, diag, 0.0)
                if m == 0:
                    piece = mine[:blk, :]
                    for k in range(1, KB):
                        piece = jnp.where(q == k, mine[k * blk : (k + 1) * blk, :], piece)
                    piece = piece.T
                    if l == 0:
                        piece = jnp.where((row_id == col_id) & (ri < ci), 0.0, piece)
                    got = jnp.where(q < KB, piece, got)
                if l == 0:
                    got = jnp.where((row_id < KB) & (col_id > row_id), 0.0, got)
                out_ref[pl.ds(l * part + m, blk, stride=wide), :] = got
        span = pl.ds(g * pair * part, pair * part)
        store = pltpu.make_async_copy(out_ref.at[span, :], out_hbm.at[span, :], out_sem.at[g])
        store.start()
        stores.append(store)
    for store in stores:
        store.wait()


def factor_call(diag, count):
    blk = diag.shape[1]
    size = KB * blk
    return pl.pallas_call(
        factor_kernel,
        out_shape=(
            jax.ShapeDtypeStruct((size, size), jnp.float32),
            jax.ShapeDtypeStruct((count, size), jnp.float32),
        ),
        out_specs=(pl.BlockSpec(memory_space=pltpu.HBM), pl.BlockSpec(memory_space=pltpu.VMEM)),
        scratch_shapes=[
            pltpu.VMEM((size, size), jnp.float32),
            pltpu.VMEM((size, size), jnp.float32),
            pltpu.VMEM((blk, 2 * blk), jnp.float32),
            pltpu.SemaphoreType.DMA((KB,)),
        ],
        compiler_params=pltpu.CompilerParams(vmem_limit_bytes=4 << 20),
        name="factor",
    )(diag)


def finish_call(place, x, mask, support, rhs, rows, cols, inv, found):
    rows_dev, blk = support.shape
    size = inv.shape[0]
    wide = x.shape[0] // (rows_dev * blk)
    scalars = pl.BlockSpec(memory_space=pltpu.SMEM)
    far = pl.BlockSpec(memory_space=pltpu.HBM)
    near = pl.BlockSpec(memory_space=pltpu.VMEM)
    return pl.pallas_call(
        finish_kernel,
        in_specs=[scalars] + [far] * 6 + [near] * 2,
        out_specs=(far, near),
        out_shape=(
            jax.ShapeDtypeStruct(x.shape, jnp.float32),
            jax.ShapeDtypeStruct(rhs.shape, jnp.float32),
        ),
        scratch_shapes=[
            pltpu.VMEM(x.shape, jnp.float32),
            pltpu.VMEM(cols.shape, jnp.float32),
            pltpu.VMEM(inv.shape, jnp.float32),
            pltpu.VMEM(rhs.shape, jnp.float32),
            pltpu.VMEM(mask.shape, jnp.int32),
            pltpu.VMEM(support.shape, jnp.float32),
            pltpu.VMEM(x.shape, jnp.float32),
            pltpu.VMEM((size, rows_dev * blk), jnp.float32),
            pltpu.VMEM((size, wide * blk), jnp.float32),
            pltpu.SemaphoreType.DMA((6,)),
            pltpu.SemaphoreType.DMA((rows_dev // 2,)),
        ],
        compiler_params=pltpu.CompilerParams(vmem_limit_bytes=14 << 20),
        name="finish",
    )(
        place,
        x,
        cols,
        pltpu.with_memory_space_constraint(inv, pltpu.HBM),
        rhs,
        mask,
        support,
        rows,
        found,
    )


def kept(mask_ref, row_id, q, n_col, wide):
    blk = mask_ref.shape[1]
    lane = lax.broadcasted_iota(jnp.int32, (wide, blk), 1)
    col_id = lax.broadcasted_iota(jnp.int32, (wide, blk), 0) * n_col + q
    own = jnp.broadcast_to(mask_ref[pl.ds(row_id, 1), :], (wide, blk)).astype(jnp.float32)
    keep = jnp.sum(jnp.where(lane == col_id, own, 0.0), axis=1, keepdims=True)
    return jnp.broadcast_to(keep, (wide, blk))


def start_kernel(
    where_ref, x_hbm, rhs_hbm, mask_hbm, support_hbm, out_ref, x_ref, rhs_ref, mask_ref,
    support_ref, sems,
):
    p = where_ref[0]
    q = where_ref[1]
    n_col = where_ref[3]
    blk = support_ref.shape[1]
    n_row, pitch = out_ref.shape[0], out_ref.shape[1]
    wide = x_ref.shape[0] // blk
    sub = blk // n_row
    pairs = (
        (mask_hbm, mask_ref), (support_hbm, support_ref), (rhs_hbm, rhs_ref),
        (x_hbm.at[pl.ds(0, blk * wide), :], x_ref),
    )
    loads = [pltpu.make_async_copy(src, dst, sems.at[i]) for i, (src, dst) in enumerate(pairs)]
    for load in loads:
        load.start()
    for load in loads[:3]:
        load.wait()
    lane = lax.broadcasted_iota(jnp.int32, (wide, blk), 1)
    col_id = lax.broadcasted_iota(jnp.int32, (wide, blk), 0) * n_col + q
    keep = kept(mask_ref, p, q, n_col, wide)
    added = jnp.where(col_id == p, jnp.broadcast_to(support_ref[0:1, :], (wide, blk)), 0.0)
    step = rhs_ref.shape[0] // n_row
    first = rhs_ref[pl.ds(0, n_row, stride=step), :]
    zero = jnp.zeros((pitch - sub * wide - 1, blk), jnp.float32)
    loads[3].wait()
    for r in range(n_row):
        for s in range(sub):
            a = r * sub + s
            got = x_ref[a * wide : (a + 1) * wide, :] * keep + jnp.where(lane == a, added, 0.0)
            out_ref[r, s * wide : (s + 1) * wide, :] = got
        out_ref[r, sub * wide :, :] = jnp.concatenate([first[r : r + 1, :], zero], axis=0)


def start_call(place, x, rhs, mask, support, n_row, wide):
    blk = support.shape[1]
    far = pl.BlockSpec(memory_space=pltpu.HBM)
    pitch = blk // n_row * wide + 8
    return pl.pallas_call(
        start_kernel,
        in_specs=[pl.BlockSpec(memory_space=pltpu.SMEM), far, far, far, far],
        out_specs=pl.BlockSpec(memory_space=pltpu.VMEM),
        out_shape=jax.ShapeDtypeStruct((n_row, pitch, blk), jnp.float32),
        scratch_shapes=[
            pltpu.VMEM((blk * wide, blk), jnp.float32),
            pltpu.VMEM(rhs.shape, jnp.float32),
            pltpu.VMEM(mask.shape, jnp.int32),
            pltpu.VMEM(support.shape, jnp.float32),
            pltpu.SemaphoreType.DMA((4,)),
        ],
        compiler_params=pltpu.CompilerParams(vmem_limit_bytes=4 << 20),
        name="start",
    )(place, x, rhs, mask, support)


def shards(front, support, mask, rhs):
    n_row = lax.axis_size("row")
    n_col = lax.axis_size("col")
    p = lax.axis_index("row")
    q = lax.axis_index("col")
    rows_dev = front.shape[0]
    blk = front.shape[2]
    cols_dev = front.shape[3]
    halves = n_row // n_col
    sub = blk // n_row
    count = rhs.shape[0]
    place = jnp.stack([p, q, jnp.int32(n_row), jnp.int32(n_col)])
    x = pltpu.with_memory_space_constraint(
        front.reshape(rows_dev * blk * cols_dev, blk), pltpu.HBM
    )
    mask = pltpu.with_memory_space_constraint(mask, pltpu.HBM)
    support = pltpu.with_memory_space_constraint(support.reshape(rows_dev, blk), pltpu.HBM)
    values = pltpu.with_memory_space_constraint(rhs.reshape(count * rows_dev, blk), pltpu.HBM)

    sent = start_call(place, x, values, mask, support, n_row, cols_dev)
    got = lax.all_to_all(sent, "row", 0, 0)[:KB]
    mine = got[:, : sub * cols_dev].reshape(KB, sub, cols_dev, blk).transpose(1, 0, 2, 3)
    mine = mine.reshape(sub * KB * cols_dev, blk)
    mine_rhs = got[:, sub * cols_dev]

    def to_all(part):
        sent = jnp.broadcast_to(part[None], (n_row,) + part.shape)
        return lax.all_to_all(sent, "row", 0, 0).reshape(-1, blk)

    cols_got = to_all(mine)
    every = lax.all_gather(mine, "col").reshape(n_col, sub, KB, rows_dev, halves, blk)
    pieces = [every[k:KB, :, k, 0, 0].transpose(1, 0, 2) for k in range(KB)]
    ends = jnp.pad(mine_rhs[:, None, :], ((0, sub - KB), (0, 1), (0, 0)))
    diag_part = jnp.concatenate(pieces + [ends], axis=1).reshape(-1, blk)
    diag_part, cols_got = lax.optimization_barrier((diag_part, cols_got))
    diag_got = to_all(diag_part)
    to_rows = every.transpose(4, 0, 1, 2, 3, 5).reshape(n_row, sub * KB * rows_dev, blk)
    rows_got = lax.all_to_all(to_rows, "row", 0, 0).reshape(-1, blk)

    inv, found = factor_call(diag_got, count)
    factor, solved = finish_call(
        place, x, mask, support, values, rows_got, cols_got, inv, found
    )
    return (factor.reshape(front.shape), solved.reshape(rhs.shape))


def solution(mesh):
    placed = (
        P(None, "row", None, None, "col", None),
        P(None, "row", None),
        P(),
        P("col", None, "row", None),
    )
    return jax.shard_map(
        shards,
        mesh=mesh,
        in_specs=placed,
        out_specs=(P(None, "row", None, None, "col", None), P("col", None, "row", None)),
        check_vma=False,
    )
```

```python
import jax
import jax.numpy as jnp
from jax import lax
from jax.experimental import pallas as pl
from jax.experimental.pallas import tpu as pltpu
from jax.sharding import PartitionSpec as P

KB = 3
SPAN = 64
STEP = 8
UPPER = KB * (KB + 1) // 2
FIRST = (
    ((0, 1), (1, 2), (2, 9)),
    ((0, 2), (1, 9), (2, 0)),
    ((0, 9), (1, 0), (2, 1)),
)
SECOND = (
    ((2, 3), (9, 8), (0, 15), (1, 6)),
    ((2, 4), (9, 10), (0, 14), (1, 7)),
    ((2, 5), (9, 11), (0, 13), (1, 12)),
)

precise = lax.Precision.HIGHEST


def tdot(a, b):
    return lax.dot_general(
        a, b, (((0,), (0,)), ((), ())), precision=precise, preferred_element_type=jnp.float32
    )


def ndot(a, b):
    return jnp.dot(a, b, precision=precise, preferred_element_type=jnp.float32)


def rdot(a, b):
    return lax.dot_general(
        a, b, (((1,), (1,)), ((), ())), precision=precise, preferred_element_type=jnp.float32
    )


def spread(x, row):
    return jnp.broadcast_to(x[row : row + 1, :], x.shape)


def eliminate_diagonal(aug_ref):
    blk = aug_ref.shape[0]
    sub = lax.broadcasted_iota(jnp.int32, (STEP, blk), 0)
    parts = SPAN // STEP
    for g in range(blk // SPAN):
        base = g * SPAN
        rows = [slice(base + STEP * j, base + STEP * (j + 1)) for j in range(parts)]
        left = [aug_ref[rows[j], :blk] for j in range(parts)]
        right = [aug_ref[rows[j], blk:] for j in range(parts)]
        for i in range(parts):
            c0 = base + STEP * i

            def columns(j):
                return [
                    jnp.broadcast_to(left[j][:, c0 + u : c0 + u + 1], (STEP, blk))
                    for u in range(STEP)
                ]

            cols = columns(i)
            pivots = jnp.ones((STEP, blk), jnp.float32)
            pairs = []
            for t in range(0, STEP, 2):
                a, b = spread(cols[t], t), spread(cols[t], t + 1)
                c = spread(cols[t + 1], t + 1)
                det = a * c - b * b
                rdet = 1.0 / det
                ra = 1.0 / a
                pivots = jnp.where(sub == t, a, jnp.where(sub == t + 1, det * ra, pivots))
                below = sub > t + 1
                m0 = jnp.where(below, (c * cols[t] - b * cols[t + 1]) * rdet, 0.0)
                m1 = jnp.where(below, (a * cols[t + 1] - b * cols[t]) * rdet, 0.0)
                tops = {}
                for u in range(t + 2, STEP):
                    tops[u] = spread(cols[u], t), spread(cols[u], t + 1)
                    cols[u] = cols[u] - (m0 * tops[u][0] + m1 * tops[u][1])
                lt = spread(left[i], t), spread(left[i], t + 1)
                rt = spread(right[i], t), spread(right[i], t + 1)
                m0 = jnp.where(sub == t + 1, b * ra, m0)
                left[i] = left[i] - (m0 * lt[0] + m1 * lt[1])
                right[i] = right[i] - (m0 * rt[0] + m1 * rt[1])
                pairs.append((a, b, c, rdet, tops, lt, rt))
            for j in range(i + 1, parts):
                cols = columns(j)
                for n, (a, b, c, rdet, tops, lt, rt) in enumerate(pairs):
                    t = 2 * n
                    m0 = (c * cols[t] - b * cols[t + 1]) * rdet
                    m1 = (a * cols[t + 1] - b * cols[t]) * rdet
                    for u in range(t + 2, STEP):
                        cols[u] = cols[u] - (m0 * tops[u][0] + m1 * tops[u][1])
                    left[j] = left[j] - (m0 * lt[0] + m1 * lt[1])
                    right[j] = right[j] - (m0 * rt[0] + m1 * rt[1])
            scale = lax.rsqrt(pivots)
            left[i] = left[i] * scale
            right[i] = right[i] * scale
        for j in range(parts):
            aug_ref[rows[j], :blk] = left[j]
            aug_ref[rows[j], blk:] = right[j]
        end = base + SPAN
        if end < blk:
            done = aug_ref[base:end, :]
            term = tdot(done[:, :blk], done)
            aug_ref[end:, :] = aug_ref[end:, :] - term[end:, :]


def factor_kernel(diag_ref, inv_hbm, found_ref, inv_ref, a_ref, aug_ref, sem):
    blk = aug_ref.shape[0]
    size = inv_ref.shape[0]
    count = found_ref.shape[0]
    pitch = diag_ref.shape[0] // blk
    base = pitch - UPPER - 2
    t = base
    for k in range(KB):
        for j in range(k, KB):
            a_ref[k * blk : (k + 1) * blk, j * blk : (j + 1) * blk] = diag_ref[
                pl.ds(t, blk, stride=pitch), :
            ]
            t += 1
    inv_ref[...] = jnp.zeros(inv_ref.shape, jnp.float32)
    eye = lax.broadcasted_iota(jnp.int32, (blk, blk), 0) == lax.broadcasted_iota(
        jnp.int32, (blk, blk), 1
    )
    stores = []
    for k in range(KB):
        k0, k1 = k * blk, (k + 1) * blk
        aug_ref[:, :blk] = a_ref[k0:k1, k0:k1]
        aug_ref[:, blk:] = eye.astype(jnp.float32)
        eliminate_diagonal(aug_ref)
        own = aug_ref[:, blk:]
        if k > 0:
            inv_ref[k0:k1, :k0] = ndot(own, inv_ref[k0:k1, :k0])
        inv_ref[k0:k1, k0:k1] = own
        store = pltpu.make_async_copy(inv_ref.at[k0:k1, :], inv_hbm.at[k0:k1, :], sem.at[k])
        store.start()
        stores.append(store)
        if k1 < size:
            up = ndot(own, a_ref[k0:k1, k1:])
            a_ref[k1:, k1:] = a_ref[k1:, k1:] - tdot(up, up)
            inv_ref[k1:, :k1] = inv_ref[k1:, :k1] - tdot(up, inv_ref[k0:k1, :k1])
    first = jnp.concatenate(
        [
            diag_ref[pl.ds(k * pitch + base + UPPER, count, stride=diag_ref.shape[0] // count), :]
            for k in range(KB)
        ],
        axis=1,
    )
    found_ref[...] = rdot(first, inv_ref[...])
    for store in stores:
        store.wait()


def gather(got_ref, wide, pitch, to_ref):
    blk = got_ref.shape[1]
    for k in range(KB):
        for j in range(wide):
            to_ref[k * blk : (k + 1) * blk, j * blk : (j + 1) * blk] = got_ref[
                pl.ds(k * wide + j, blk, stride=pitch), :
            ]


def solve(inv_ref, to_ref, blk):
    for k in reversed(range(KB)):
        k0, k1 = k * blk, (k + 1) * blk
        to_ref[k0:k1, :] = ndot(inv_ref[k0:k1, :k1], to_ref[:k1, :])


def finish_kernel(
    where_ref, x_hbm, cols_hbm, inv_hbm, rhs_hbm, mask_hbm, support_hbm, rows_ref, found_ref,
    out_hbm, solved_ref, x_ref, cols_ref, inv_ref, rhs_ref, mask_ref, support_ref, out_ref,
    row_ref, col_ref, sems, out_sem,
):
    p = where_ref[0]
    q = where_ref[1]
    n_row = where_ref[2]
    n_col = where_ref[3]
    rows_dev, blk = support_ref.shape
    wide = col_ref.shape[1] // blk
    count = found_ref.shape[0]
    part = blk * wide
    loads = [
        pltpu.make_async_copy(src, dst, sems.at[i])
        for i, (src, dst) in enumerate(
            ((inv_hbm, inv_ref), (cols_hbm, cols_ref), (x_hbm, x_ref), (rhs_hbm, rhs_ref),
             (mask_hbm, mask_ref), (support_hbm, support_ref))
        )
    ]
    for load in loads:
        load.start()
    gather(rows_ref, rows_dev, KB * rows_dev, row_ref)
    loads[0].wait()
    solve(inv_ref, row_ref, blk)
    loads[3].wait()
    rest = ndot(found_ref[...], row_ref[...])
    for l in range(rows_dev):
        got = rhs_ref[pl.ds(l, count, stride=rows_dev), :] - rest[:, l * blk : (l + 1) * blk]
        if l == 0:
            for k in range(KB):
                got = jnp.where(p == k, found_ref[:, k * blk : (k + 1) * blk], got)
        solved_ref[pl.ds(l, count, stride=rows_dev), :] = got

    loads[1].wait()
    gather(cols_ref, wide, cols_ref.shape[0] // blk, col_ref)
    solve(inv_ref, col_ref, blk)
    ri = lax.broadcasted_iota(jnp.int32, (blk, blk), 0)
    ci = lax.broadcasted_iota(jnp.int32, (blk, blk), 1)
    loads[4].wait()
    loads[5].wait()
    loads[2].wait()
    stores = []
    pair = 2
    for g in range(rows_dev // pair):
        term = tdot(row_ref[:, g * pair * blk : (g + 1) * pair * blk], col_ref[...])
        for h in range(pair):
            l = g * pair + h
            mine = row_ref[:, l * blk : (l + 1) * blk]
            row_id = l * n_row + p
            keep = kept(mask_ref, row_id, q, n_col, wide)
            diag = jnp.where(
                ri == ci, jnp.broadcast_to(support_ref[l : l + 1, :], (blk, blk)), 0.0
            )
            for m in range(wide):
                col_id = m * n_col + q
                got = x_ref[pl.ds(l * part + m, blk, stride=wide), :]
                got = got * jnp.broadcast_to(keep[m : m + 1, :], (blk, blk))
                got = got - term[h * blk : (h + 1) * blk, m * blk : (m + 1) * blk]
                got = got + jnp.where(row_id == col_id, diag, 0.0)
                if m == 0:
                    piece = mine[:blk, :]
                    for k in range(1, KB):
                        piece = jnp.where(q == k, mine[k * blk : (k + 1) * blk, :], piece)
                    piece = piece.T
                    if l == 0:
                        piece = jnp.where((row_id == col_id) & (ri < ci), 0.0, piece)
                    got = jnp.where(q < KB, piece, got)
                if l == 0:
                    got = jnp.where((row_id < KB) & (col_id > row_id), 0.0, got)
                out_ref[pl.ds(l * part + m, blk, stride=wide), :] = got
        span = pl.ds(g * pair * part, pair * part)
        store = pltpu.make_async_copy(out_ref.at[span, :], out_hbm.at[span, :], out_sem.at[g])
        store.start()
        stores.append(store)
    for store in stores:
        store.wait()


def factor_call(diag, count):
    blk = diag.shape[1]
    size = KB * blk
    return pl.pallas_call(
        factor_kernel,
        out_shape=(
            jax.ShapeDtypeStruct((size, size), jnp.float32),
            jax.ShapeDtypeStruct((count, size), jnp.float32),
        ),
        out_specs=(pl.BlockSpec(memory_space=pltpu.HBM), pl.BlockSpec(memory_space=pltpu.VMEM)),
        scratch_shapes=[
            pltpu.VMEM((size, size), jnp.float32),
            pltpu.VMEM((size, size), jnp.float32),
            pltpu.VMEM((blk, 2 * blk), jnp.float32),
            pltpu.SemaphoreType.DMA((KB,)),
        ],
        compiler_params=pltpu.CompilerParams(vmem_limit_bytes=4 << 20),
        name="factor",
    )(diag)


def finish_call(place, x, mask, support, rhs, rows, cols, inv, found):
    rows_dev, blk = support.shape
    size = inv.shape[0]
    wide = x.shape[0] // (rows_dev * blk)
    scalars = pl.BlockSpec(memory_space=pltpu.SMEM)
    far = pl.BlockSpec(memory_space=pltpu.HBM)
    near = pl.BlockSpec(memory_space=pltpu.VMEM)
    return pl.pallas_call(
        finish_kernel,
        in_specs=[scalars] + [far] * 6 + [near] * 2,
        out_specs=(far, near),
        out_shape=(
            jax.ShapeDtypeStruct(x.shape, jnp.float32),
            jax.ShapeDtypeStruct(rhs.shape, jnp.float32),
        ),
        scratch_shapes=[
            pltpu.VMEM(x.shape, jnp.float32),
            pltpu.VMEM(cols.shape, jnp.float32),
            pltpu.VMEM(inv.shape, jnp.float32),
            pltpu.VMEM(rhs.shape, jnp.float32),
            pltpu.VMEM(mask.shape, jnp.int32),
            pltpu.VMEM(support.shape, jnp.float32),
            pltpu.VMEM(x.shape, jnp.float32),
            pltpu.VMEM((size, rows_dev * blk), jnp.float32),
            pltpu.VMEM((size, wide * blk), jnp.float32),
            pltpu.SemaphoreType.DMA((6,)),
            pltpu.SemaphoreType.DMA((rows_dev // 2,)),
        ],
        compiler_params=pltpu.CompilerParams(vmem_limit_bytes=14 << 20),
        name="finish",
    )(
        place,
        x,
        cols,
        pltpu.with_memory_space_constraint(inv, pltpu.HBM),
        rhs,
        mask,
        support,
        rows,
        found,
    )


def kept(mask_ref, row_id, q, n_col, wide):
    blk = mask_ref.shape[1]
    lane = lax.broadcasted_iota(jnp.int32, (wide, blk), 1)
    col_id = lax.broadcasted_iota(jnp.int32, (wide, blk), 0) * n_col + q
    own = jnp.broadcast_to(mask_ref[pl.ds(row_id, 1), :], (wide, blk)).astype(jnp.float32)
    keep = jnp.sum(jnp.where(lane == col_id, own, 0.0), axis=1, keepdims=True)
    return jnp.broadcast_to(keep, (wide, blk))


def start_kernel(
    where_ref, x_hbm, rhs_hbm, mask_hbm, support_hbm, out_ref, x_ref, rhs_ref, mask_ref,
    support_ref, sems,
):
    p = where_ref[0]
    q = where_ref[1]
    n_col = where_ref[3]
    blk = support_ref.shape[1]
    n_row, pitch = out_ref.shape[0], out_ref.shape[1]
    wide = x_ref.shape[0] // blk
    sub = blk // n_row
    pairs = (
        (mask_hbm, mask_ref), (support_hbm, support_ref), (rhs_hbm, rhs_ref),
        (x_hbm.at[pl.ds(0, blk * wide), :], x_ref),
    )
    loads = [pltpu.make_async_copy(src, dst, sems.at[i]) for i, (src, dst) in enumerate(pairs)]
    for load in loads:
        load.start()
    for load in loads[:3]:
        load.wait()
    lane = lax.broadcasted_iota(jnp.int32, (wide, blk), 1)
    col_id = lax.broadcasted_iota(jnp.int32, (wide, blk), 0) * n_col + q
    keep = kept(mask_ref, p, q, n_col, wide)
    added = jnp.where(col_id == p, jnp.broadcast_to(support_ref[0:1, :], (wide, blk)), 0.0)
    step = rhs_ref.shape[0] // n_row
    first = rhs_ref[pl.ds(0, n_row, stride=step), :]
    zero = jnp.zeros((pitch - sub * wide - 1, blk), jnp.float32)
    loads[3].wait()
    for r in range(n_row):
        for s in range(sub):
            a = r * sub + s
            got = x_ref[a * wide : (a + 1) * wide, :] * keep + jnp.where(lane == a, added, 0.0)
            out_ref[r, s * wide : (s + 1) * wide, :] = got
        out_ref[r, sub * wide :, :] = jnp.concatenate([first[r : r + 1, :], zero], axis=0)


def start_call(place, x, rhs, mask, support, n_row, wide):
    blk = support.shape[1]
    far = pl.BlockSpec(memory_space=pltpu.HBM)
    pitch = blk // n_row * wide + 8
    return pl.pallas_call(
        start_kernel,
        in_specs=[pl.BlockSpec(memory_space=pltpu.SMEM), far, far, far, far],
        out_specs=pl.BlockSpec(memory_space=pltpu.VMEM),
        out_shape=jax.ShapeDtypeStruct((n_row, pitch, blk), jnp.float32),
        scratch_shapes=[
            pltpu.VMEM((blk * wide, blk), jnp.float32),
            pltpu.VMEM(rhs.shape, jnp.float32),
            pltpu.VMEM(mask.shape, jnp.int32),
            pltpu.VMEM(support.shape, jnp.float32),
            pltpu.SemaphoreType.DMA((4,)),
        ],
        compiler_params=pltpu.CompilerParams(vmem_limit_bytes=4 << 20),
        name="start",
    )(place, x, rhs, mask, support)


def at_col(q, k):
    return jnp.stack([(q == j).astype(jnp.float32) for j in range(k, KB)])[None, :, None]


def shards(front, support, mask, rhs):
    n_row = lax.axis_size("row")
    n_col = lax.axis_size("col")
    p = lax.axis_index("row")
    q = lax.axis_index("col")
    rows_dev = front.shape[0]
    blk = front.shape[2]
    cols_dev = front.shape[3]
    halves = n_row // n_col
    sub = blk // n_row
    count = rhs.shape[0]
    place = jnp.stack([p, q, jnp.int32(n_row), jnp.int32(n_col)])
    x = pltpu.with_memory_space_constraint(
        front.reshape(rows_dev * blk * cols_dev, blk), pltpu.HBM
    )
    mask = pltpu.with_memory_space_constraint(mask, pltpu.HBM)
    support = pltpu.with_memory_space_constraint(support.reshape(rows_dev, blk), pltpu.HBM)
    values = pltpu.with_memory_space_constraint(rhs.reshape(count * rows_dev, blk), pltpu.HBM)

    sent = start_call(place, x, values, mask, support, n_row, cols_dev)
    got = lax.all_to_all(sent, "row", 0, 0)[:KB]
    mine = got[:, : sub * cols_dev].reshape(KB, sub, cols_dev, blk).transpose(1, 0, 2, 3)
    mine = mine.reshape(sub * KB * cols_dev, blk)
    mine_rhs = got[:, sub * cols_dev]

    corner = mine.reshape(sub, KB, cols_dev, blk)[:, :, 0]
    own = jnp.concatenate(
        [corner[:, k : k + 1] * at_col(q, k) for k in range(KB)], axis=1
    )
    own = jnp.pad(own, ((0, 0), (0, 2), (0, 0)))
    hub = own
    for pairs in FIRST:
        hub = hub + lax.ppermute(own, "col", pairs)
    corner = hub
    for pairs in SECOND:
        corner = corner + lax.ppermute(hub, "col", pairs)
    corner = corner + jnp.pad(mine_rhs[:, None, :], ((0, sub - KB), (UPPER, 1), (0, 0)))

    part = jnp.concatenate([mine.reshape(sub, KB * cols_dev, blk), corner], axis=1)
    part = part.reshape(-1, blk)
    mine, part = lax.optimization_barrier((mine, part))
    sent = jnp.broadcast_to(part[None], (n_row,) + part.shape)
    cols_got = lax.all_to_all(sent, "row", 0, 0).reshape(-1, blk)
    every = lax.all_gather(mine, "col").reshape(n_col, sub, KB, rows_dev, halves, blk)
    to_rows = every.transpose(4, 0, 1, 2, 3, 5).reshape(n_row, sub * KB * rows_dev, blk)
    to_rows, cols_got = lax.optimization_barrier((to_rows, cols_got))
    rows_got = lax.all_to_all(to_rows, "row", 0, 0).reshape(-1, blk)

    inv, found = factor_call(cols_got, count)
    factor, solved = finish_call(
        place, x, mask, support, values, rows_got, cols_got, inv, found
    )
    return (factor.reshape(front.shape), solved.reshape(rhs.shape))


def solution(mesh):
    placed = (
        P(None, "row", None, None, "col", None),
        P(None, "row", None),
        P(),
        P("col", None, "row", None),
    )
    return jax.shard_map(
        shards,
        mesh=mesh,
        in_specs=placed,
        out_specs=(P(None, "row", None, None, "col", None), P("col", None, "row", None)),
        check_vma=False,
    )
```

```python
import jax
import jax.numpy as jnp
from jax import lax
from jax.experimental import pallas as pl
from jax.experimental.pallas import tpu as pltpu
from jax.sharding import PartitionSpec as P

KB = 3
SPAN = 64
STEP = 8
UPPER = KB * (KB + 1) // 2

precise = lax.Precision.HIGHEST


def tdot(a, b):
    return lax.dot_general(
        a, b, (((0,), (0,)), ((), ())), precision=precise, preferred_element_type=jnp.float32
    )


def ndot(a, b):
    return jnp.dot(a, b, precision=precise, preferred_element_type=jnp.float32)


def rdot(a, b):
    return lax.dot_general(
        a, b, (((1,), (1,)), ((), ())), precision=precise, preferred_element_type=jnp.float32
    )


def spread(x, row):
    return jnp.broadcast_to(x[row : row + 1, :], x.shape)


def eliminate_diagonal(aug_ref):
    blk = aug_ref.shape[0]
    sub = lax.broadcasted_iota(jnp.int32, (STEP, blk), 0)
    parts = SPAN // STEP
    for g in range(blk // SPAN):
        base = g * SPAN
        rows = [slice(base + STEP * j, base + STEP * (j + 1)) for j in range(parts)]
        left = [aug_ref[rows[j], :blk] for j in range(parts)]
        right = [aug_ref[rows[j], blk:] for j in range(parts)]
        for i in range(parts):
            c0 = base + STEP * i

            def columns(j):
                return [
                    jnp.broadcast_to(left[j][:, c0 + u : c0 + u + 1], (STEP, blk))
                    for u in range(STEP)
                ]

            cols = columns(i)
            pivots = jnp.ones((STEP, blk), jnp.float32)
            pairs = []
            for t in range(0, STEP, 2):
                a, b = spread(cols[t], t), spread(cols[t], t + 1)
                c = spread(cols[t + 1], t + 1)
                det = a * c - b * b
                rdet = 1.0 / det
                ra = 1.0 / a
                pivots = jnp.where(sub == t, a, jnp.where(sub == t + 1, det * ra, pivots))
                below = sub > t + 1
                m0 = jnp.where(below, (c * cols[t] - b * cols[t + 1]) * rdet, 0.0)
                m1 = jnp.where(below, (a * cols[t + 1] - b * cols[t]) * rdet, 0.0)
                tops = {}
                for u in range(t + 2, STEP):
                    tops[u] = spread(cols[u], t), spread(cols[u], t + 1)
                    cols[u] = cols[u] - (m0 * tops[u][0] + m1 * tops[u][1])
                lt = spread(left[i], t), spread(left[i], t + 1)
                rt = spread(right[i], t), spread(right[i], t + 1)
                m0 = jnp.where(sub == t + 1, b * ra, m0)
                left[i] = left[i] - (m0 * lt[0] + m1 * lt[1])
                right[i] = right[i] - (m0 * rt[0] + m1 * rt[1])
                pairs.append((a, b, c, rdet, tops, lt, rt))
            for j in range(i + 1, parts):
                cols = columns(j)
                for n, (a, b, c, rdet, tops, lt, rt) in enumerate(pairs):
                    t = 2 * n
                    m0 = (c * cols[t] - b * cols[t + 1]) * rdet
                    m1 = (a * cols[t + 1] - b * cols[t]) * rdet
                    for u in range(t + 2, STEP):
                        cols[u] = cols[u] - (m0 * tops[u][0] + m1 * tops[u][1])
                    left[j] = left[j] - (m0 * lt[0] + m1 * lt[1])
                    right[j] = right[j] - (m0 * rt[0] + m1 * rt[1])
            scale = lax.rsqrt(pivots)
            left[i] = left[i] * scale
            right[i] = right[i] * scale
        for j in range(parts):
            aug_ref[rows[j], :blk] = left[j]
            aug_ref[rows[j], blk:] = right[j]
        end = base + SPAN
        if end < blk:
            done = aug_ref[base:end, :]
            term = tdot(done[:, :blk], done)
            aug_ref[end:, :] = aug_ref[end:, :] - term[end:, :]


def factor_kernel(diag_ref, inv_hbm, found_ref, inv_ref, a_ref, aug_ref, sem):
    blk = aug_ref.shape[0]
    size = inv_ref.shape[0]
    count = found_ref.shape[0]
    pitch = UPPER + 2
    t = 0
    for k in range(KB):
        for j in range(k, KB):
            a_ref[k * blk : (k + 1) * blk, j * blk : (j + 1) * blk] = diag_ref[
                pl.ds(t, blk, stride=pitch), :
            ]
            t += 1
    inv_ref[...] = jnp.zeros(inv_ref.shape, jnp.float32)
    eye = lax.broadcasted_iota(jnp.int32, (blk, blk), 0) == lax.broadcasted_iota(
        jnp.int32, (blk, blk), 1
    )
    stores = []
    for k in range(KB):
        k0, k1 = k * blk, (k + 1) * blk
        aug_ref[:, :blk] = a_ref[k0:k1, k0:k1]
        aug_ref[:, blk:] = eye.astype(jnp.float32)
        eliminate_diagonal(aug_ref)
        own = aug_ref[:, blk:]
        if k > 0:
            inv_ref[k0:k1, :k0] = ndot(own, inv_ref[k0:k1, :k0])
        inv_ref[k0:k1, k0:k1] = own
        store = pltpu.make_async_copy(inv_ref.at[k0:k1, :], inv_hbm.at[k0:k1, :], sem.at[k])
        store.start()
        stores.append(store)
        if k1 < size:
            up = ndot(own, a_ref[k0:k1, k1:])
            a_ref[k1:, k1:] = a_ref[k1:, k1:] - tdot(up, up)
            inv_ref[k1:, :k1] = inv_ref[k1:, :k1] - tdot(up, inv_ref[k0:k1, :k1])
    first = jnp.concatenate(
        [
            diag_ref[pl.ds(k * pitch + UPPER, count, stride=diag_ref.shape[0] // count), :]
            for k in range(KB)
        ],
        axis=1,
    )
    found_ref[...] = rdot(first, inv_ref[...])
    for store in stores:
        store.wait()


def gather(got_ref, wide, to_ref):
    blk = got_ref.shape[1]
    for k in range(KB):
        for j in range(wide):
            to_ref[k * blk : (k + 1) * blk, j * blk : (j + 1) * blk] = got_ref[
                pl.ds(k * wide + j, blk, stride=KB * wide), :
            ]


def solve(inv_ref, to_ref, blk):
    for k in reversed(range(KB)):
        k0, k1 = k * blk, (k + 1) * blk
        to_ref[k0:k1, :] = ndot(inv_ref[k0:k1, :k1], to_ref[:k1, :])


def finish_kernel(
    where_ref, x_hbm, cols_hbm, inv_hbm, rhs_hbm, mask_hbm, support_hbm, rows_ref, found_ref,
    out_hbm, solved_ref, x_ref, cols_ref, inv_ref, rhs_ref, mask_ref, support_ref, out_ref,
    row_ref, col_ref, sems, out_sem,
):
    p = where_ref[0]
    q = where_ref[1]
    n_row = where_ref[2]
    n_col = where_ref[3]
    rows_dev, blk = support_ref.shape
    wide = col_ref.shape[1] // blk
    count = found_ref.shape[0]
    part = blk * wide
    loads = [
        pltpu.make_async_copy(src, dst, sems.at[i])
        for i, (src, dst) in enumerate(
            ((inv_hbm, inv_ref), (cols_hbm, cols_ref), (x_hbm, x_ref), (rhs_hbm, rhs_ref),
             (mask_hbm, mask_ref), (support_hbm, support_ref))
        )
    ]
    for load in loads:
        load.start()
    gather(rows_ref, rows_dev, row_ref)
    loads[0].wait()
    solve(inv_ref, row_ref, blk)
    loads[3].wait()
    rest = ndot(found_ref[...], row_ref[...])
    for l in range(rows_dev):
        got = rhs_ref[pl.ds(l, count, stride=rows_dev), :] - rest[:, l * blk : (l + 1) * blk]
        if l == 0:
            for k in range(KB):
                got = jnp.where(p == k, found_ref[:, k * blk : (k + 1) * blk], got)
        solved_ref[pl.ds(l, count, stride=rows_dev), :] = got

    loads[1].wait()
    gather(cols_ref, wide, col_ref)
    solve(inv_ref, col_ref, blk)
    ri = lax.broadcasted_iota(jnp.int32, (blk, blk), 0)
    ci = lax.broadcasted_iota(jnp.int32, (blk, blk), 1)
    loads[4].wait()
    loads[5].wait()
    loads[2].wait()
    stores = []
    pair = 1
    for g in range(rows_dev // pair):
        term = tdot(row_ref[:, g * pair * blk : (g + 1) * pair * blk], col_ref[...])
        for h in range(pair):
            l = g * pair + h
            mine = row_ref[:, l * blk : (l + 1) * blk]
            row_id = l * n_row + p
            keep = kept(mask_ref, row_id, q, n_col, wide)
            diag = jnp.where(
                ri == ci, jnp.broadcast_to(support_ref[l : l + 1, :], (blk, blk)), 0.0
            )
            for m in range(wide):
                col_id = m * n_col + q
                got = x_ref[pl.ds(l * part + m, blk, stride=wide), :]
                got = got * jnp.broadcast_to(keep[m : m + 1, :], (blk, blk))
                got = got - term[h * blk : (h + 1) * blk, m * blk : (m + 1) * blk]
                got = got + jnp.where(row_id == col_id, diag, 0.0)
                if m == 0:
                    piece = mine[:blk, :]
                    for k in range(1, KB):
                        piece = jnp.where(q == k, mine[k * blk : (k + 1) * blk, :], piece)
                    piece = piece.T
                    if l == 0:
                        piece = jnp.where((row_id == col_id) & (ri < ci), 0.0, piece)
                    got = jnp.where(q < KB, piece, got)
                if l == 0:
                    got = jnp.where((row_id < KB) & (col_id > row_id), 0.0, got)
                out_ref[pl.ds(l * part + m, blk, stride=wide), :] = got
        span = pl.ds(g * pair * part, pair * part)
        store = pltpu.make_async_copy(out_ref.at[span, :], out_hbm.at[span, :], out_sem.at[g])
        store.start()
        stores.append(store)
    for store in stores:
        store.wait()


def factor_call(diag, count):
    blk = diag.shape[1]
    size = KB * blk
    return pl.pallas_call(
        factor_kernel,
        out_shape=(
            pltpu.HBM((size, size), jnp.float32),
            jax.ShapeDtypeStruct((count, size), jnp.float32),
        ),
        out_specs=(pl.BlockSpec(memory_space=pltpu.HBM), pl.BlockSpec(memory_space=pltpu.VMEM)),
        scratch_shapes=[
            pltpu.VMEM((size, size), jnp.float32),
            pltpu.VMEM((size, size), jnp.float32),
            pltpu.VMEM((blk, 2 * blk), jnp.float32),
            pltpu.SemaphoreType.DMA((KB,)),
        ],
        compiler_params=pltpu.CompilerParams(vmem_limit_bytes=4 << 20),
        name="factor",
    )(diag)


def finish_call(place, x, mask, support, rhs, rows, cols, inv, found):
    rows_dev, blk = support.shape
    size = inv.shape[0]
    wide = x.shape[0] // (rows_dev * blk)
    scalars = pl.BlockSpec(memory_space=pltpu.SMEM)
    far = pl.BlockSpec(memory_space=pltpu.HBM)
    near = pl.BlockSpec(memory_space=pltpu.VMEM)
    return pl.pallas_call(
        finish_kernel,
        in_specs=[scalars] + [far] * 6 + [near] * 2,
        out_specs=(far, near),
        out_shape=(
            jax.ShapeDtypeStruct(x.shape, jnp.float32),
            jax.ShapeDtypeStruct(rhs.shape, jnp.float32),
        ),
        scratch_shapes=[
            pltpu.VMEM(x.shape, jnp.float32),
            pltpu.VMEM(cols.shape, jnp.float32),
            pltpu.VMEM(inv.shape, jnp.float32),
            pltpu.VMEM(rhs.shape, jnp.float32),
            pltpu.VMEM(mask.shape, jnp.int32),
            pltpu.VMEM(support.shape, jnp.float32),
            pltpu.VMEM(x.shape, jnp.float32),
            pltpu.VMEM((size, rows_dev * blk), jnp.float32),
            pltpu.VMEM((size, wide * blk), jnp.float32),
            pltpu.SemaphoreType.DMA((6,)),
            pltpu.SemaphoreType.DMA((rows_dev,)),
        ],
        compiler_params=pltpu.CompilerParams(vmem_limit_bytes=14 << 20),
        name="finish",
    )(
        place,
        x,
        cols,
        pltpu.with_memory_space_constraint(inv, pltpu.HBM),
        rhs,
        mask,
        support,
        rows,
        found,
    )


def kept(mask_ref, row_id, q, n_col, wide):
    blk = mask_ref.shape[1]
    lane = lax.broadcasted_iota(jnp.int32, (wide, blk), 1)
    col_id = lax.broadcasted_iota(jnp.int32, (wide, blk), 0) * n_col + q
    own = jnp.broadcast_to(mask_ref[pl.ds(row_id, 1), :], (wide, blk)).astype(jnp.float32)
    keep = jnp.sum(jnp.where(lane == col_id, own, 0.0), axis=1, keepdims=True)
    return jnp.broadcast_to(keep, (wide, blk))


def start_kernel(
    where_ref, x_hbm, rhs_hbm, mask_hbm, support_hbm, out_ref, x_ref, rhs_ref, mask_ref,
    support_ref, sems,
):
    p = where_ref[0]
    q = where_ref[1]
    n_col = where_ref[3]
    blk = support_ref.shape[1]
    n_row, pitch = out_ref.shape[0], out_ref.shape[1]
    wide = x_ref.shape[0] // blk
    sub = blk // n_row
    pairs = (
        (mask_hbm, mask_ref), (support_hbm, support_ref), (rhs_hbm, rhs_ref),
        (x_hbm.at[pl.ds(0, blk * wide), :], x_ref),
    )
    loads = [pltpu.make_async_copy(src, dst, sems.at[i]) for i, (src, dst) in enumerate(pairs)]
    for load in loads:
        load.start()
    for load in loads[:3]:
        load.wait()
    lane = lax.broadcasted_iota(jnp.int32, (wide, blk), 1)
    col_id = lax.broadcasted_iota(jnp.int32, (wide, blk), 0) * n_col + q
    keep = kept(mask_ref, p, q, n_col, wide)
    added = jnp.where(col_id == p, jnp.broadcast_to(support_ref[0:1, :], (wide, blk)), 0.0)
    step = rhs_ref.shape[0] // n_row
    first = rhs_ref[pl.ds(0, n_row, stride=step), :]
    zero = jnp.zeros((pitch - sub * wide - 1, blk), jnp.float32)
    loads[3].wait()
    for r in range(n_row):
        for s in range(sub):
            a = r * sub + s
            got = x_ref[a * wide : (a + 1) * wide, :] * keep + jnp.where(lane == a, added, 0.0)
            out_ref[r, s * wide : (s + 1) * wide, :] = got
        out_ref[r, sub * wide :, :] = jnp.concatenate([first[r : r + 1, :], zero], axis=0)


def start_call(place, x, rhs, mask, support, n_row, wide):
    blk = support.shape[1]
    far = pl.BlockSpec(memory_space=pltpu.HBM)
    pitch = blk // n_row * wide + 8
    return pl.pallas_call(
        start_kernel,
        in_specs=[pl.BlockSpec(memory_space=pltpu.SMEM), far, far, far, far],
        out_specs=pl.BlockSpec(memory_space=pltpu.VMEM),
        out_shape=jax.ShapeDtypeStruct((n_row, pitch, blk), jnp.float32),
        scratch_shapes=[
            pltpu.VMEM((blk * wide, blk), jnp.float32),
            pltpu.VMEM(rhs.shape, jnp.float32),
            pltpu.VMEM(mask.shape, jnp.int32),
            pltpu.VMEM(support.shape, jnp.float32),
            pltpu.SemaphoreType.DMA((4,)),
        ],
        compiler_params=pltpu.CompilerParams(vmem_limit_bytes=4 << 20),
        name="start",
    )(place, x, rhs, mask, support)


def shards(front, support, mask, rhs):
    n_row = lax.axis_size("row")
    n_col = lax.axis_size("col")
    p = lax.axis_index("row")
    q = lax.axis_index("col")
    rows_dev = front.shape[0]
    blk = front.shape[2]
    cols_dev = front.shape[3]
    halves = n_row // n_col
    sub = blk // n_row
    count = rhs.shape[0]
    place = jnp.stack([p, q, jnp.int32(n_row), jnp.int32(n_col)])
    x = pltpu.with_memory_space_constraint(
        front.reshape(rows_dev * blk * cols_dev, blk), pltpu.HBM
    )
    mask = pltpu.with_memory_space_constraint(mask, pltpu.HBM)
    support = pltpu.with_memory_space_constraint(support.reshape(rows_dev, blk), pltpu.HBM)
    values = pltpu.with_memory_space_constraint(rhs.reshape(count * rows_dev, blk), pltpu.HBM)

    sent = start_call(place, x, values, mask, support, n_row, cols_dev)
    got = lax.all_to_all(sent, "row", 0, 0)[:KB]
    mine = got[:, : sub * cols_dev].reshape(KB, sub, cols_dev, blk).transpose(1, 0, 2, 3)
    mine = mine.reshape(sub * KB * cols_dev, blk)
    mine_rhs = got[:, sub * cols_dev]

    def to_all(part):
        sent = jnp.broadcast_to(part[None], (n_row,) + part.shape)
        return lax.all_to_all(sent, "row", 0, 0).reshape(-1, blk)

    cols_got = to_all(mine)
    every = lax.all_gather(mine, "col").reshape(n_col, sub, KB, rows_dev, halves, blk)
    pieces = [every[k:KB, :, k, 0, 0].transpose(1, 0, 2) for k in range(KB)]
    ends = jnp.pad(mine_rhs[:, None, :], ((0, sub - KB), (0, 1), (0, 0)))
    diag_part = jnp.concatenate(pieces + [ends], axis=1).reshape(-1, blk)
    diag_part, cols_got = lax.optimization_barrier((diag_part, cols_got))
    diag_got = to_all(diag_part)
    to_rows = every.transpose(4, 0, 1, 2, 3, 5).reshape(n_row, sub * KB * rows_dev, blk)
    rows_got = lax.all_to_all(to_rows, "row", 0, 0).reshape(-1, blk)

    inv, found = factor_call(diag_got, count)
    factor, solved = finish_call(
        place, x, mask, support, values, rows_got, cols_got, inv, found
    )
    return (factor.reshape(front.shape), solved.reshape(rhs.shape))


def solution(mesh):
    placed = (
        P(None, "row", None, None, "col", None),
        P(None, "row", None),
        P(),
        P("col", None, "row", None),
    )
    return jax.shard_map(
        shards,
        mesh=mesh,
        in_specs=placed,
        out_specs=(P(None, "row", None, None, "col", None), P("col", None, "row", None)),
        check_vma=False,
    )
```

```python
import jax
import jax.numpy as jnp
from jax import lax
from jax.experimental import pallas as pl
from jax.experimental.pallas import tpu as pltpu
from jax.sharding import PartitionSpec as P

KB = 3
SPAN = 64
STEP = 8
UPPER = KB * (KB + 1) // 2

precise = lax.Precision.HIGHEST


def tdot(a, b):
    return lax.dot_general(
        a, b, (((0,), (0,)), ((), ())), precision=precise, preferred_element_type=jnp.float32
    )


def ndot(a, b):
    return jnp.dot(a, b, precision=precise, preferred_element_type=jnp.float32)


def rdot(a, b):
    return lax.dot_general(
        a, b, (((1,), (1,)), ((), ())), precision=precise, preferred_element_type=jnp.float32
    )


def spread(x, row):
    return jnp.broadcast_to(x[row : row + 1, :], x.shape)


def eliminate_diagonal(aug_ref):
    blk = aug_ref.shape[0]
    sub = lax.broadcasted_iota(jnp.int32, (STEP, blk), 0)
    parts = SPAN // STEP
    for g in range(blk // SPAN):
        base = g * SPAN
        rows = [slice(base + STEP * j, base + STEP * (j + 1)) for j in range(parts)]
        left = [aug_ref[rows[j], :blk] for j in range(parts)]
        right = [aug_ref[rows[j], blk:] for j in range(parts)]
        for i in range(parts):
            c0 = base + STEP * i

            def columns(j):
                return [
                    jnp.broadcast_to(left[j][:, c0 + u : c0 + u + 1], (STEP, blk))
                    for u in range(STEP)
                ]

            cols = columns(i)
            pivots = jnp.ones((STEP, blk), jnp.float32)
            pairs = []
            for t in range(0, STEP, 2):
                a, b = spread(cols[t], t), spread(cols[t], t + 1)
                c = spread(cols[t + 1], t + 1)
                det = a * c - b * b
                rdet = 1.0 / det
                ra = 1.0 / a
                pivots = jnp.where(sub == t, a, jnp.where(sub == t + 1, det * ra, pivots))
                below = sub > t + 1
                m0 = jnp.where(below, (c * cols[t] - b * cols[t + 1]) * rdet, 0.0)
                m1 = jnp.where(below, (a * cols[t + 1] - b * cols[t]) * rdet, 0.0)
                tops = {}
                for u in range(t + 2, STEP):
                    tops[u] = spread(cols[u], t), spread(cols[u], t + 1)
                    cols[u] = cols[u] - (m0 * tops[u][0] + m1 * tops[u][1])
                lt = spread(left[i], t), spread(left[i], t + 1)
                rt = spread(right[i], t), spread(right[i], t + 1)
                m0 = jnp.where(sub == t + 1, b * ra, m0)
                left[i] = left[i] - (m0 * lt[0] + m1 * lt[1])
                right[i] = right[i] - (m0 * rt[0] + m1 * rt[1])
                pairs.append((a, b, c, rdet, tops, lt, rt))
            for j in range(i + 1, parts):
                cols = columns(j)
                for n, (a, b, c, rdet, tops, lt, rt) in enumerate(pairs):
                    t = 2 * n
                    m0 = (c * cols[t] - b * cols[t + 1]) * rdet
                    m1 = (a * cols[t + 1] - b * cols[t]) * rdet
                    for u in range(t + 2, STEP):
                        cols[u] = cols[u] - (m0 * tops[u][0] + m1 * tops[u][1])
                    left[j] = left[j] - (m0 * lt[0] + m1 * lt[1])
                    right[j] = right[j] - (m0 * rt[0] + m1 * rt[1])
            scale = lax.rsqrt(pivots)
            left[i] = left[i] * scale
            right[i] = right[i] * scale
        for j in range(parts):
            aug_ref[rows[j], :blk] = left[j]
            aug_ref[rows[j], blk:] = right[j]
        end = base + SPAN
        if end < blk:
            done = aug_ref[base:end, :]
            term = tdot(done[:, :blk], done)
            aug_ref[end:, :] = aug_ref[end:, :] - term[end:, :]


def factor_kernel(diag_ref, inv_hbm, found_ref, inv_ref, a_ref, aug_ref, sem):
    blk = aug_ref.shape[0]
    size = inv_ref.shape[0]
    count = found_ref.shape[0]
    pitch = UPPER + 2
    t = 0
    for k in range(KB):
        for j in range(k, KB):
            a_ref[k * blk : (k + 1) * blk, j * blk : (j + 1) * blk] = diag_ref[
                pl.ds(t, blk, stride=pitch), :
            ]
            t += 1
    inv_ref[...] = jnp.zeros(inv_ref.shape, jnp.float32)
    eye = lax.broadcasted_iota(jnp.int32, (blk, blk), 0) == lax.broadcasted_iota(
        jnp.int32, (blk, blk), 1
    )
    stores = []
    for k in range(KB):
        k0, k1 = k * blk, (k + 1) * blk
        aug_ref[:, :blk] = a_ref[k0:k1, k0:k1]
        aug_ref[:, blk:] = eye.astype(jnp.float32)
        eliminate_diagonal(aug_ref)
        own = aug_ref[:, blk:]
        if k > 0:
            inv_ref[k0:k1, :k0] = ndot(own, inv_ref[k0:k1, :k0])
        inv_ref[k0:k1, k0:k1] = own
        store = pltpu.make_async_copy(inv_ref.at[k0:k1, :], inv_hbm.at[k0:k1, :], sem.at[k])
        store.start()
        stores.append(store)
        if k1 < size:
            up = ndot(own, a_ref[k0:k1, k1:])
            a_ref[k1:, k1:] = a_ref[k1:, k1:] - tdot(up, up)
            inv_ref[k1:, :k1] = inv_ref[k1:, :k1] - tdot(up, inv_ref[k0:k1, :k1])
    first = jnp.concatenate(
        [
            diag_ref[pl.ds(k * pitch + UPPER, count, stride=diag_ref.shape[0] // count), :]
            for k in range(KB)
        ],
        axis=1,
    )
    found_ref[...] = rdot(first, inv_ref[...])
    for store in stores:
        store.wait()


def gather(got_ref, wide, to_ref):
    blk = got_ref.shape[1]
    for k in range(KB):
        for j in range(wide):
            to_ref[k * blk : (k + 1) * blk, j * blk : (j + 1) * blk] = got_ref[
                pl.ds(k * wide + j, blk, stride=KB * wide), :
            ]


def solve(inv_ref, to_ref, blk):
    for k in reversed(range(KB)):
        k0, k1 = k * blk, (k + 1) * blk
        to_ref[k0:k1, :] = ndot(inv_ref[k0:k1, :k1], to_ref[:k1, :])


def finish_kernel(
    where_ref, x_hbm, cols_hbm, inv_hbm, rhs_hbm, mask_hbm, support_hbm, rows_ref, found_ref,
    out_hbm, solved_ref, x_ref, cols_ref, inv_ref, rhs_ref, mask_ref, support_ref, out_ref,
    row_ref, col_ref, sems, out_sem,
):
    p = where_ref[0]
    q = where_ref[1]
    n_row = where_ref[2]
    n_col = where_ref[3]
    rows_dev, blk = support_ref.shape
    wide = col_ref.shape[1] // blk
    count = found_ref.shape[0]
    part = blk * wide
    loads = [
        pltpu.make_async_copy(src, dst, sems.at[i])
        for i, (src, dst) in enumerate(
            ((inv_hbm, inv_ref), (cols_hbm, cols_ref), (x_hbm, x_ref), (rhs_hbm, rhs_ref),
             (mask_hbm, mask_ref), (support_hbm, support_ref))
        )
    ]
    for load in loads:
        load.start()
    gather(rows_ref, rows_dev, row_ref)
    loads[0].wait()
    solve(inv_ref, row_ref, blk)
    loads[3].wait()
    rest = ndot(found_ref[...], row_ref[...])
    for l in range(rows_dev):
        got = rhs_ref[pl.ds(l, count, stride=rows_dev), :] - rest[:, l * blk : (l + 1) * blk]
        if l == 0:
            for k in range(KB):
                got = jnp.where(p == k, found_ref[:, k * blk : (k + 1) * blk], got)
        solved_ref[pl.ds(l, count, stride=rows_dev), :] = got

    loads[1].wait()
    gather(cols_ref, wide, col_ref)
    solve(inv_ref, col_ref, blk)
    ri = lax.broadcasted_iota(jnp.int32, (blk, blk), 0)
    ci = lax.broadcasted_iota(jnp.int32, (blk, blk), 1)
    loads[4].wait()
    loads[5].wait()
    loads[2].wait()
    stores = []
    pair = 1
    for g in range(rows_dev // pair):
        term = tdot(row_ref[:, g * pair * blk : (g + 1) * pair * blk], col_ref[...])
        for h in range(pair):
            l = g * pair + h
            mine = row_ref[:, l * blk : (l + 1) * blk]
            row_id = l * n_row + p
            keep = kept(mask_ref, row_id, q, n_col, wide)
            diag = jnp.where(
                ri == ci, jnp.broadcast_to(support_ref[l : l + 1, :], (blk, blk)), 0.0
            )
            for m in range(wide):
                col_id = m * n_col + q
                got = x_ref[pl.ds(l * part + m, blk, stride=wide), :]
                got = got * jnp.broadcast_to(keep[m : m + 1, :], (blk, blk))
                got = got - term[h * blk : (h + 1) * blk, m * blk : (m + 1) * blk]
                got = got + jnp.where(row_id == col_id, diag, 0.0)
                if m == 0:
                    piece = mine[:blk, :]
                    for k in range(1, KB):
                        piece = jnp.where(q == k, mine[k * blk : (k + 1) * blk, :], piece)
                    piece = piece.T
                    if l == 0:
                        piece = jnp.where((row_id == col_id) & (ri < ci), 0.0, piece)
                    got = jnp.where(q < KB, piece, got)
                if l == 0:
                    got = jnp.where((row_id < KB) & (col_id > row_id), 0.0, got)
                out_ref[pl.ds(l * part + m, blk, stride=wide), :] = got
        span = pl.ds(g * pair * part, pair * part)
        store = pltpu.make_async_copy(out_ref.at[span, :], out_hbm.at[span, :], out_sem.at[g])
        store.start()
        stores.append(store)
    for store in stores:
        store.wait()


def factor_call(diag, count):
    blk = diag.shape[1]
    size = KB * blk
    return pl.pallas_call(
        factor_kernel,
        out_shape=(
            pltpu.HBM((size, size), jnp.float32),
            jax.ShapeDtypeStruct((count, size), jnp.float32),
        ),
        out_specs=(pl.BlockSpec(memory_space=pltpu.HBM), pl.BlockSpec(memory_space=pltpu.VMEM)),
        scratch_shapes=[
            pltpu.VMEM((size, size), jnp.float32),
            pltpu.VMEM((size, size), jnp.float32),
            pltpu.VMEM((blk, 2 * blk), jnp.float32),
            pltpu.SemaphoreType.DMA((KB,)),
        ],
        compiler_params=pltpu.CompilerParams(vmem_limit_bytes=4 << 20),
        name="factor",
    )(diag)


def finish_call(place, x, mask, support, rhs, rows, cols, inv, found):
    rows_dev, blk = support.shape
    size = inv.shape[0]
    wide = x.shape[0] // (rows_dev * blk)
    scalars = pl.BlockSpec(memory_space=pltpu.SMEM)
    far = pl.BlockSpec(memory_space=pltpu.HBM)
    near = pl.BlockSpec(memory_space=pltpu.VMEM)
    return pl.pallas_call(
        finish_kernel,
        in_specs=[scalars] + [far] * 6 + [near] * 2,
        out_specs=(far, near),
        out_shape=(
            jax.ShapeDtypeStruct(x.shape, jnp.float32),
            jax.ShapeDtypeStruct(rhs.shape, jnp.float32),
        ),
        scratch_shapes=[
            pltpu.VMEM(x.shape, jnp.float32),
            pltpu.VMEM(cols.shape, jnp.float32),
            pltpu.VMEM(inv.shape, jnp.float32),
            pltpu.VMEM(rhs.shape, jnp.float32),
            pltpu.VMEM(mask.shape, jnp.int32),
            pltpu.VMEM(support.shape, jnp.float32),
            pltpu.VMEM(x.shape, jnp.float32),
            pltpu.VMEM((size, rows_dev * blk), jnp.float32),
            pltpu.VMEM((size, wide * blk), jnp.float32),
            pltpu.SemaphoreType.DMA((6,)),
            pltpu.SemaphoreType.DMA((rows_dev,)),
        ],
        compiler_params=pltpu.CompilerParams(vmem_limit_bytes=14 << 20),
        name="finish",
    )(
        place,
        x,
        cols,
        pltpu.with_memory_space_constraint(inv, pltpu.HBM),
        rhs,
        mask,
        support,
        rows,
        found,
    )


def kept(mask_ref, row_id, q, n_col, wide):
    blk = mask_ref.shape[1]
    lane = lax.broadcasted_iota(jnp.int32, (wide, blk), 1)
    col_id = lax.broadcasted_iota(jnp.int32, (wide, blk), 0) * n_col + q
    own = jnp.broadcast_to(mask_ref[pl.ds(row_id, 1), :], (wide, blk)).astype(jnp.float32)
    keep = jnp.sum(jnp.where(lane == col_id, own, 0.0), axis=1, keepdims=True)
    return jnp.broadcast_to(keep, (wide, blk))


def start_kernel(
    where_ref, x_hbm, rhs_hbm, mask_hbm, support_hbm, out_ref, x_ref, rhs_ref, mask_ref,
    support_ref, sems,
):
    p = where_ref[0]
    q = where_ref[1]
    n_col = where_ref[3]
    blk = support_ref.shape[1]
    n_row, pitch = out_ref.shape[0], out_ref.shape[1]
    wide = x_ref.shape[0] // blk
    sub = blk // n_row
    pairs = (
        (mask_hbm, mask_ref), (support_hbm, support_ref), (rhs_hbm, rhs_ref),
        (x_hbm.at[pl.ds(0, blk * wide), :], x_ref),
    )
    loads = [pltpu.make_async_copy(src, dst, sems.at[i]) for i, (src, dst) in enumerate(pairs)]
    for load in loads:
        load.start()
    for load in loads[:3]:
        load.wait()
    lane = lax.broadcasted_iota(jnp.int32, (wide, blk), 1)
    col_id = lax.broadcasted_iota(jnp.int32, (wide, blk), 0) * n_col + q
    keep = kept(mask_ref, p, q, n_col, wide)
    added = jnp.where(col_id == p, jnp.broadcast_to(support_ref[0:1, :], (wide, blk)), 0.0)
    step = rhs_ref.shape[0] // n_row
    first = rhs_ref[pl.ds(0, n_row, stride=step), :]
    zero = jnp.zeros((pitch - sub * wide - 1, blk), jnp.float32)
    loads[3].wait()
    for r in range(n_row):
        for s in range(sub):
            a = r * sub + s
            got = x_ref[a * wide : (a + 1) * wide, :] * keep + jnp.where(lane == a, added, 0.0)
            out_ref[r, s * wide : (s + 1) * wide, :] = got
        out_ref[r, sub * wide :, :] = jnp.concatenate([first[r : r + 1, :], zero], axis=0)


def start_call(place, x, rhs, mask, support, n_row, wide):
    blk = support.shape[1]
    far = pl.BlockSpec(memory_space=pltpu.HBM)
    pitch = blk // n_row * wide + 8
    return pl.pallas_call(
        start_kernel,
        in_specs=[pl.BlockSpec(memory_space=pltpu.SMEM), far, far, far, far],
        out_specs=pl.BlockSpec(memory_space=pltpu.VMEM),
        out_shape=jax.ShapeDtypeStruct((n_row, pitch, blk), jnp.float32),
        scratch_shapes=[
            pltpu.VMEM((blk * wide, blk), jnp.float32),
            pltpu.VMEM(rhs.shape, jnp.float32),
            pltpu.VMEM(mask.shape, jnp.int32),
            pltpu.VMEM(support.shape, jnp.float32),
            pltpu.SemaphoreType.DMA((4,)),
        ],
        compiler_params=pltpu.CompilerParams(vmem_limit_bytes=4 << 20),
        name="start",
    )(place, x, rhs, mask, support)


def shards(front, support, mask, rhs):
    n_row = lax.axis_size("row")
    n_col = lax.axis_size("col")
    p = lax.axis_index("row")
    q = lax.axis_index("col")
    rows_dev = front.shape[0]
    blk = front.shape[2]
    cols_dev = front.shape[3]
    halves = n_row // n_col
    sub = blk // n_row
    count = rhs.shape[0]
    place = jnp.stack([p, q, jnp.int32(n_row), jnp.int32(n_col)])
    x = pltpu.with_memory_space_constraint(
        front.reshape(rows_dev * blk * cols_dev, blk), pltpu.HBM
    )
    mask = pltpu.with_memory_space_constraint(mask, pltpu.HBM)
    support = pltpu.with_memory_space_constraint(support.reshape(rows_dev, blk), pltpu.HBM)
    values = pltpu.with_memory_space_constraint(rhs.reshape(count * rows_dev, blk), pltpu.HBM)

    sent = start_call(place, x, values, mask, support, n_row, cols_dev)
    got = lax.all_to_all(sent, "row", 0, 0)[:KB]
    mine = got[:, : sub * cols_dev].reshape(KB, sub, cols_dev, blk).transpose(1, 0, 2, 3)
    mine = mine.reshape(sub * KB * cols_dev, blk)
    mine_rhs = got[:, sub * cols_dev]

    def to_all(part):
        sent = jnp.broadcast_to(part[None], (n_row,) + part.shape)
        return lax.all_to_all(sent, "row", 0, 0).reshape(-1, blk)

    cols_got = to_all(mine)
    every = lax.all_gather(mine, "col")
    pieces = [every[k:KB, k * cols_dev :: KB * cols_dev].transpose(1, 0, 2) for k in range(KB)]
    ends = jnp.pad(mine_rhs[:, None, :], ((0, sub - KB), (0, 1), (0, 0)))
    diag_part = jnp.concatenate(pieces + [ends], axis=1).reshape(-1, blk)
    diag_part, cols_got, every = lax.optimization_barrier((diag_part, cols_got, every))
    diag_got = to_all(diag_part)
    every = every.reshape(n_col, sub, KB, rows_dev, halves, blk)
    to_rows = every.transpose(4, 0, 1, 2, 3, 5).reshape(n_row, sub * KB * rows_dev, blk)
    rows_got = lax.all_to_all(to_rows, "row", 0, 0).reshape(-1, blk)

    inv, found = factor_call(diag_got, count)
    factor, solved = finish_call(
        place, x, mask, support, values, rows_got, cols_got, inv, found
    )
    return (factor.reshape(front.shape), solved.reshape(rhs.shape))


def solution(mesh):
    placed = (
        P(None, "row", None, None, "col", None),
        P(None, "row", None),
        P(),
        P("col", None, "row", None),
    )
    return jax.shard_map(
        shards,
        mesh=mesh,
        in_specs=placed,
        out_specs=(P(None, "row", None, None, "col", None), P("col", None, "row", None)),
        check_vma=False,
    )
```
